32 devices in a mesh: video: 2 (over x), seq: 8 (over z, y), head: 2 (over core).
Axes of the slice: x: 2, y: 2, z: 4, core: 2. Of those that a mesh axis runs over, the one named last changes fastest.
Arguments:
- query: bfloat16 [6144, 1536], P(('video', 'seq'), 'head'), parts along dimension 0, may hold values from -5 to 5
- key: bfloat16 [6144, 1536], P(('video', 'seq'), 'head'), parts along dimension 0, may hold values from -5 to 5
- value: bfloat16 [6144, 1536], P(('video', 'seq'), 'head'), parts along dimension 0, may hold values from -6 to 6
- stream: bfloat16 [6144, 3072], P(('video', 'seq'), 'head'), parts along dimension 0, may hold values from -12 to 12
- shift_mod: float32 [6144], P('video'), parts along dimension 0, may hold values from -3 to 3
- scale_mod: float32 [6144], P('video'), parts along dimension 0, may hold values from -3 to 3
- out_weight: bfloat16 [1536, 3072], P('seq', 'head'), may hold values from -0.5 to 0.5
Outputs:
- normed: bfloat16 [6144, 3072], P(('video', 'seq'), 'head'), parts along dimension 0
- stream_out: bfloat16 [6144, 3072], P(('video', 'seq'), 'head'), parts along dimension 0
The draws below stay inside these ranges and needn't reach their ends.
There are 2 independent parts, one for each index of `video`. The reference program is written for one: setup_inputs(seed, part) draws one part's arguments, and reference() takes and returns one part's arrays. A program takes and returns all parts, laid end to end along the dimension named above; an argument that names none is the same for every part. Nothing has to cross between parts.
All inputs are finite; a program needn't handle non-finite values.
Results may differ from the reference program's by a relative error of at most 0.0051.
Values may be sent and summed in bfloat16 or wider, within the bound.
No kernel may reach another device: no remote copies, remote signals or barrier semaphores. Data moves between devices by JAX's collectives and lax.ppermute only.
A program may use at most 128 MiB of HBM per device.

```python
import math
import jax
import jax.numpy as jnp
from jax import lax

D = 3072
HEADS = 12
HD = 128
TILE = 128
WT = 3
HT = 4
TT = 2
TOKENS = 3072


def drawn_pair(key):
    features = HEADS * HD
    base_query = jnp.clip(1.2 * jax.random.normal(jax.random.fold_in(key, 101), (TOKENS, features), jnp.float32), -4.8, 4.8)
    base_key = jnp.clip(1.2 * jax.random.normal(jax.random.fold_in(key, 102), (TOKENS, features), jnp.float32), -4.8, 4.8)
    return (base_query, base_key)


def draw_query(key, part):
    return drawn_pair(key)[0].astype(jnp.bfloat16)


def draw_key(key, part):
    return drawn_pair(key)[1].astype(jnp.bfloat16)


def draw_stream(key, part):
    base = jnp.clip(jax.random.normal(jax.random.fold_in(key, 201), (TOKENS, D), jnp.float32), -4.0, 4.0)
    column_ramp = 1.0 + 2.0 * jnp.arange(D, dtype=jnp.float32) / D
    column_scale = jnp.exp(jax.random.uniform(jax.random.fold_in(key, 202), (D,), jnp.float32, math.log(0.05), 0.0)) * column_ramp
    row_scale = jnp.exp(jax.random.uniform(jax.random.fold_in(key, 203), (TOKENS,), jnp.float32, math.log(0.2), 0.0))
    return (base * column_scale[None, :] * row_scale[:, None]).astype(jnp.bfloat16)


def steps_of(rng, dims, split, low, high):
    def one(axis_at, parts):
        steps = jax.random.uniform(jax.random.fold_in(jax.random.fold_in(rng, 6), axis_at), (parts,), jnp.float32, low / len(split), high / len(split))
        return jnp.repeat(jnp.exp(steps), dims[axis_at] // parts).reshape((-1,) + (1,) * (len(dims) - axis_at - 1))

    loudness = one(*split[0])
    for cut in split[1:]:
        loudness = loudness * one(*cut)
    return loudness


def noise(own_key, dims, scale, limit, shards=(), kind=jnp.bfloat16):
    level = steps_of(own_key, dims, shards, -0.22, 0.18) if shards else 1.0
    entries = jax.random.normal(own_key, dims, jnp.float32) * scale * level
    return jnp.minimum(jnp.maximum(entries, -limit), limit).astype(kind)


def setup_inputs(seed: int = 0, part: int = 0) -> dict:
    arg_keys = jax.random.split(jax.random.key(seed), 8)
    part_splits = jax.random.split(jax.random.fold_in(arg_keys[7], part), 8)
    return {
        "query": draw_query(jax.random.fold_in(jax.random.fold_in(arg_keys[7], part), 71), part),
        "key": draw_key(jax.random.fold_in(jax.random.fold_in(arg_keys[7], part), 71), part),
        "value": noise(part_splits[2], (TOKENS, HEADS * HD), 1.0, 6.0, ((0, 8), (1, 2))),
        "stream": draw_stream(jax.random.fold_in(jax.random.fold_in(arg_keys[7], part), 71), part),
        "shift_mod": noise(part_splits[4], (D,), 0.5, 3.0, (), jnp.float32),
        "scale_mod": noise(part_splits[5], (D,), 0.5, 3.0, (), jnp.float32),
        "out_weight": noise(arg_keys[6], (HEADS * HD, D), HD ** -0.5, 0.5, ((0, 8), (1, 2))),
    }


def reference(query, key, value, stream, shift_mod, scale_mod, out_weight):
    slab = WT * TILE
    layer_rows = HT * slab
    shape_four = (TT, layer_rows, HEADS, HD)
    padding = ((1, 1), (0, 0), (0, 0), (0, 0))
    query_layers = query.reshape(shape_four)
    key_layers = jnp.pad(key.reshape(shape_four), padding)
    value_layers = jnp.pad(value.reshape(shape_four), padding)
    rows = jnp.arange(layer_rows, dtype=jnp.int32)
    height = rows // slab
    width = rows // TILE % WT
    key_height = jnp.tile(height, 3)
    key_width = jnp.tile(width, 3)
    near = (jnp.abs(height[:, None] - key_height[None, :]) <= 1) & (jnp.abs(width[:, None] - key_width[None, :]) <= 1)

    def one_layer(layer):
        queries = lax.dynamic_index_in_dim(query_layers, layer, 0, keepdims=False).astype(jnp.float32)
        keys_here = lax.dynamic_slice_in_dim(key_layers, layer, 3, 0).reshape(3 * layer_rows, HEADS, HD).astype(jnp.float32)
        values_here = lax.dynamic_slice_in_dim(value_layers, layer, 3, 0).reshape(3 * layer_rows, HEADS, HD).astype(jnp.float32)
        key_time = layer - 1 + jnp.arange(3 * layer_rows, dtype=jnp.int32) // layer_rows
        visible = near & ((key_time >= 0) & (key_time < TT))[None, :]

        def one_head(head):
            head_query = lax.dynamic_index_in_dim(queries, head, 1, keepdims=False)
            head_key = lax.dynamic_index_in_dim(keys_here, head, 1, keepdims=False)
            head_value = lax.dynamic_index_in_dim(values_here, head, 1, keepdims=False)
            scores = jnp.dot(head_query, head_key.T, preferred_element_type=jnp.float32) / math.sqrt(HD)
            scores = jnp.where(visible, scores, -jnp.inf)
            top = lax.optimization_barrier(jnp.max(scores, axis=1, keepdims=True))
            expo = jnp.exp(scores - top)
            total = lax.optimization_barrier(jnp.sum(expo, axis=1, keepdims=True))
            probs = lax.optimization_barrier(expo.astype(jnp.bfloat16)).astype(jnp.float32)
            weighted = jnp.dot(probs, head_value, preferred_element_type=jnp.float32)
            return (weighted / total).astype(jnp.bfloat16)
        per_head = lax.map(one_head, jnp.arange(HEADS, dtype=jnp.int32))
        return jnp.transpose(per_head, (1, 0, 2))
    attended = lax.map(one_layer, jnp.arange(TT, dtype=jnp.int32)).reshape(TOKENS, HEADS * HD)
    mixed = stream.astype(jnp.float32) + jnp.dot(attended, out_weight, preferred_element_type=jnp.float32)
    mean = lax.optimization_barrier(jnp.mean(mixed, axis=1, keepdims=True))
    centered = mixed - mean
    var = lax.optimization_barrier(jnp.mean(centered * centered, axis=1, keepdims=True))
    normed = (centered * lax.rsqrt(var + 1e-06) * (1.0 + scale_mod) + shift_mod).astype(jnp.bfloat16)
    return (normed, mixed.astype(jnp.bfloat16))
```

```python
import functools
import math

import jax
import jax.numpy as jnp
from jax import lax
from jax.experimental import pallas as pl
from jax.experimental.pallas import tpu as pltpu
from jax.sharding import PartitionSpec as P

D = 3072
HD = 128
TILE = 128
HT = 4
EPS = 1e-06
EXP2_SCALE = math.log2(math.e) / math.sqrt(HD)
AWAY = -1e30


def shifted(value, axis, steps):
    count = lax.axis_size(axis)
    leading, last = (max(0, -steps), min(count, count - steps))
    return lax.ppermute(value, axis, [(source, source + steps) for source in range(leading, last)])


def attend_tile(query_tile, keys_all, values_all, visible):
    tile_rows, features = query_tile.shape
    heads_here = features // HD

    def one_head(head):
        head_query = lax.dynamic_slice_in_dim(query_tile, head * HD, HD, 1)
        head_key = lax.dynamic_slice_in_dim(keys_all, head * HD, HD, 1)
        head_value = lax.dynamic_slice_in_dim(values_all, head * HD, HD, 1)
        scores = jnp.einsum(
            "nd,md->nm", head_query, head_key, preferred_element_type=jnp.float32
        ) / math.sqrt(HD)
        scores = jnp.where(visible[None, :], scores, -jnp.inf)
        top = jnp.max(scores, axis=1, keepdims=True)
        expo = jnp.exp(scores - top)
        total = jnp.sum(expo, axis=1, keepdims=True)
        probs = expo.astype(jnp.bfloat16)
        weighted = jnp.dot(probs, head_value, preferred_element_type=jnp.float32)
        return (weighted / total).astype(jnp.bfloat16)

    per_head = lax.map(one_head, jnp.arange(heads_here, dtype=jnp.int32))
    return jnp.transpose(per_head, (1, 0, 2)).reshape(tile_rows, features)


def on_device_any(query, key, value, stream, shift_mod, scale_mod, out_weight):
    slab_rows = query.shape[0]
    width_tiles = slab_rows // TILE
    layers = lax.axis_size("seq") // HT
    position = lax.axis_index("seq")
    time_tile = position // HT
    height_tile = position % HT
    key_value = jnp.stack([key, value])
    vertical = {0: key_value}
    for offset in (HT, -HT):
        vertical[-offset // HT] = shifted(key_value, "seq", offset)
    column = jnp.stack([vertical[-1], vertical[0], vertical[1]])
    sideways = {0: column}
    for offset in (1, -1):
        sideways[-offset] = shifted(column, "seq", offset)
    neighbours = []
    for across in (-1, 0, 1):
        for upward in (-1, 0, 1):
            inside = (time_tile + across >= 0) & (time_tile + across < layers)
            inside = inside & (height_tile + upward >= 0) & (height_tile + upward < HT)
            neighbours.append((sideways[upward][across + 1], inside))
    results = []
    for tile_pos in range(width_tiles):
        lowest = max(tile_pos - 1, 0)
        highest = min(tile_pos + 1, width_tiles - 1)
        begin = lowest * TILE
        count = (highest - lowest + 1) * TILE
        keys_here = jnp.concatenate(
            [paired[0][begin : begin + count] for paired, inside in neighbours], 0
        )
        values_here = jnp.concatenate(
            [paired[1][begin : begin + count] for paired, inside in neighbours], 0
        )
        flags = jnp.concatenate(
            [jnp.broadcast_to(inside, (count,)) for paired, inside in neighbours]
        )
        query_tile = query[tile_pos * TILE : (tile_pos + 1) * TILE]
        results.append(attend_tile(query_tile, keys_here, values_here, flags))
    attended = jnp.concatenate(results, 0)
    width_cols = D // lax.axis_size("head")
    first_col = lax.axis_index("head") * width_cols
    weight_cols = lax.all_gather(out_weight, "seq", axis=0, tiled=True)
    weight_rows = lax.all_to_all(weight_cols, "head", split_axis=0, concat_axis=1, tiled=True)
    partial_value = jnp.dot(attended, weight_rows, preferred_element_type=jnp.float32)
    share = lax.psum_scatter(partial_value, "head", scatter_dimension=1, tiled=True)
    mixed = stream.astype(jnp.float32) + share
    totals, squares = lax.psum((jnp.sum(mixed, axis=1), jnp.sum(mixed * mixed, axis=1)), "head")
    mean = (totals / D)[:, None]
    var = (squares / D)[:, None] - mean * mean
    scale_part = lax.dynamic_slice_in_dim(scale_mod, first_col, width_cols, 0)
    shift_part = lax.dynamic_slice_in_dim(shift_mod, first_col, width_cols, 0)
    normed = ((mixed - mean) * lax.rsqrt(var + EPS) * (1.0 + scale_part) + shift_part).astype(
        jnp.bfloat16
    )
    return (normed, mixed.astype(jnp.bfloat16))


def attention_kernel(info, query, c0, c1, y0, y1, z0, z1, out):
    rows = query.shape[0]
    tiles = rows // TILE
    away = jnp.where(info[1] == 1, jnp.float32(0), jnp.float32(AWAY))
    parts = ((c0, False), (c1, False), (y0, False), (y1, False), (z0, True), (z1, True))
    for tile in range(tiles):
        begin = max(tile - 1, 0) * TILE
        end = (min(tile + 1, tiles - 1) + 1) * TILE
        q = query[tile * TILE : (tile + 1) * TILE, :]
        scores = []
        tops = []
        for part, far in parts:
            s = lax.dot_general(
                q,
                part[0, begin:end, :],
                (((1,), (1,)), ((), ())),
                preferred_element_type=jnp.float32,
            )
            scores.append(s)
            top = jnp.max(s, axis=1, keepdims=True)
            tops.append(top + away if far else top)
        top = functools.reduce(jnp.maximum, tops)
        total = jnp.zeros((TILE, 1), jnp.float32)
        acc = jnp.zeros((TILE, HD), jnp.float32)
        for s, (part, far) in zip(scores, parts):
            p = jnp.exp2((s - (top - away if far else top)) * EXP2_SCALE)
            total = total + jnp.sum(p, axis=1, keepdims=True)
            acc = acc + jnp.dot(
                p.astype(jnp.bfloat16), part[1, begin:end, :], preferred_element_type=jnp.float32
            )
        out[tile * TILE : (tile + 1) * TILE, :] = (acc / total).astype(jnp.bfloat16)


def attention(info, query, own, parts):
    rows = query.shape[0]
    cols = parts[0].shape[2]
    heads = cols // HD
    if own:
        q_map = lambda j, info: (0, info[0] * heads + j)
    else:
        q_map = lambda j, info: (0, j)
    kv_spec = pl.BlockSpec((2, rows, HD), lambda j, info: (0, 0, j))
    pairs = rows * 7 * TILE * 2 * heads
    return pl.pallas_call(
        attention_kernel,
        grid_spec=pltpu.PrefetchScalarGridSpec(
            num_scalar_prefetch=1,
            grid=(heads,),
            in_specs=[pl.BlockSpec((rows, HD), q_map)] + [kv_spec] * 6,
            out_specs=pl.BlockSpec((rows, HD), lambda j, info: (0, j)),
        ),
        out_shape=jax.ShapeDtypeStruct((rows, cols), jnp.bfloat16),
        compiler_params=pltpu.CompilerParams(vmem_limit_bytes=32 << 20),
        cost_estimate=pl.CostEstimate(
            flops=pairs * HD * 4, transcendentals=pairs, bytes_accessed=rows * cols * 28
        ),
        name="attend",
    )(info, query, *parts)


def project_kernel(
    info, a_own, a_ret, x_own, x_ret, stream, *rest, places, count
):
    pieces = rest[:count]
    mixed, stream_out, stats, weight, left, sems = rest[count:]
    core, par, pos, vid = info[0], info[1], info[2], info[3]
    copies = []
    for piece, where in zip(pieces, places):
        for slot, (flip, half, size) in enumerate(where):
            other = pos ^ flip
            if half is None:
                row = other * size
            else:
                row = other * (2 * size) + (vid if half == 0 else 1 - vid) * size
            source = piece if len(where) == 1 and len(piece.shape) == 2 else piece.at[slot]
            copy = pltpu.make_async_copy(
                source, weight.at[pl.ds(pl.multiple_of(row, 32), size)], sems.at[len(copies)]
            )
            copy.start()
            copies.append(copy)
    cols = a_own.shape[1]
    for ref, block in (
        (a_own, core * 2 + par),
        (a_ret, core * 2 + 1 - par),
        (x_own, (1 - core) * 2 + par),
        (x_ret, (1 - core) * 2 + 1 - par),
    ):
        left[:, pl.ds(pl.multiple_of(block * cols, HD), cols)] = ref[...]
    for copy in copies:
        copy.wait()
    rows, width = stream.shape
    step = 512
    total = jnp.zeros((rows, 1), jnp.float32)
    for first in range(0, width, step):
        got = jnp.dot(
            left[...], weight[:, first : first + step], preferred_element_type=jnp.float32
        ) + stream[:, first : first + step].astype(jnp.float32)
        mixed[:, first : first + step] = got
        stream_out[:, first : first + step] = got.astype(jnp.bfloat16)
        total = total + jnp.sum(got, axis=1, keepdims=True)
    mean = total * (1.0 / width)
    square = jnp.zeros((rows, 1), jnp.float32)
    for first in range(0, width, step):
        off = mixed[:, first : first + step] - mean
        square = square + jnp.sum(off * off, axis=1, keepdims=True)
    lane = lax.broadcasted_iota(jnp.int32, stats.shape, 1)
    stats[...] = jnp.where(lane == 0, mean, square)


def project(info, blocks, stream, pieces, places):
    rows, width = stream.shape
    depth = 4 * blocks[0].shape[1]
    copies = sum(len(where) for where in places)
    vmem = pl.BlockSpec(memory_space=pltpu.VMEM)
    return pl.pallas_call(
        functools.partial(project_kernel, places=places, count=len(pieces)),
        in_specs=[pl.BlockSpec(memory_space=pltpu.SMEM)]
        + [vmem] * 5
        + [pl.BlockSpec(memory_space=pl.ANY)] * len(pieces),
        out_specs=[vmem] * 3,
        out_shape=[
            jax.ShapeDtypeStruct((rows, width), jnp.float32),
            jax.ShapeDtypeStruct((rows, width), jnp.bfloat16),
            jax.ShapeDtypeStruct((rows, HD), jnp.float32),
        ],
        scratch_shapes=[
            pltpu.VMEM((depth, width), jnp.bfloat16),
            pltpu.VMEM((rows, depth), jnp.bfloat16),
            pltpu.SemaphoreType.DMA((copies,)),
        ],
        compiler_params=pltpu.CompilerParams(vmem_limit_bytes=40 << 20),
        cost_estimate=pl.CostEstimate(
            flops=2 * rows * depth * width,
            transcendentals=0,
            bytes_accessed=depth * width * 2 + rows * width * 8,
        ),
        name="project",
    )(info, *blocks, stream, *pieces)


def norm_kernel(info, mixed, mine, other, scale, shift, out, *, half):
    m0, m1 = mine[:, 0:1], other[:, 0:1]
    q0, q1 = mine[:, 1:2], other[:, 1:2]
    mean = 0.5 * (m0 + m1)
    gap = m0 - m1
    var = (q0 + q1 + gap * gap * (0.5 * half)) * (0.5 / half)
    rate = lax.rsqrt(var + EPS)
    out[...] = ((mixed[...] - mean) * rate * (1.0 + scale[...]) + shift[...]).astype(jnp.bfloat16)


def normalize(info, mixed, mine, other, scale_mod, shift_mod):
    rows, width = mixed.shape
    step = TILE
    row_block = pl.BlockSpec((step, width), lambda i, info: (i, 0))
    stat_block = pl.BlockSpec((step, HD), lambda i, info: (i, 0))
    mod_block = pl.BlockSpec((1, width), lambda i, info: (0, info[0]))
    return pl.pallas_call(
        functools.partial(norm_kernel, half=float(width)),
        grid_spec=pltpu.PrefetchScalarGridSpec(
            num_scalar_prefetch=1,
            grid=(rows // step,),
            in_specs=[row_block, stat_block, stat_block, mod_block, mod_block],
            out_specs=row_block,
        ),
        out_shape=jax.ShapeDtypeStruct((rows, width), jnp.bfloat16),
        compiler_params=pltpu.CompilerParams(vmem_limit_bytes=24 << 20),
        cost_estimate=pl.CostEstimate(
            flops=6 * rows * width, transcendentals=rows, bytes_accessed=rows * width * 6
        ),
        name="normalize",
    )(info, mixed, mine, other, scale_mod[None, :], shift_mod[None, :])


def after(value, *done):
    return lax.optimization_barrier((value,) + done)[0]


def on_device_pair(query, key, value, stream, shift_mod, scale_mod, out_weight):
    count = lax.axis_size("seq")
    position = lax.axis_index("seq")
    core = lax.axis_index("head")
    vid = lax.axis_index("video")
    par = position // HT
    height = position % HT
    relayed = jnp.where((height == 1) | (height == 2), 1, 0)
    half_cols = query.shape[1] // 2

    def flip(x, mask):
        return lax.ppermute(x, "seq", [(i, i ^ mask) for i in range(count)])

    def swap(x, axis):
        return lax.ppermute(x, axis, [(0, 1), (1, 0)])

    def relay(x):
        pairs = []
        for i in range(count):
            if i % HT == 0:
                pairs.append((i, i + 2))
            if i % HT == 3:
                pairs.append((i, i - 2))
        return lax.ppermute(x, "seq", pairs)

    def heads(x, which):
        return lax.dynamic_slice_in_dim(x, which * half_cols, half_cols, 1)

    give = jnp.stack([heads(key, 1 - par), heads(value, 1 - par)])
    give_q = heads(query, 1 - par)
    own = jnp.stack([heads(key, par), heads(value, par)])
    rows_half = out_weight.shape[0] // 2
    w_own = lax.dynamic_slice_in_dim(out_weight, vid * rows_half, rows_half, 0)

    got = flip(give, HT)
    y_own = flip(own, 1)
    w_z1 = flip(w_own, 2)
    z_own = relay(y_own)
    w_y1 = flip(after(jnp.stack([w_own, w_z1]), y_own), 1)
    w_x1 = swap(jnp.concatenate([w_z1[None], w_y1]), "video")
    y_oth = flip(got, 1)
    w_t = flip(after(w_own, got), HT)
    z_oth = relay(y_oth)
    got_q = flip(after(give_q, w_t), HT)
    w_z2 = flip(w_t, 2)
    w_two = jnp.stack([w_t, w_z2])
    w_y2 = flip(after(w_two, y_oth), 1)
    w_x2 = swap(w_two, "video")
    w_x3 = swap(w_y2, "video")

    info = jnp.stack([par, relayed]).astype(jnp.int32)
    parts = (own, got, y_own, y_oth, z_own, z_oth)
    out_other = attention(info, got_q, False, parts)
    a_ret = flip(out_other, HT)
    a_own = attention(info, query, True, parts)
    x_own = swap(a_own, "head")
    x_ret = swap(a_ret, "head")

    n = rows_half
    pieces = (out_weight, w_z1, w_y1, w_x1, w_t, w_z2, w_y2, w_x2, w_x3)
    places = (
        ((0, None, 2 * n),),
        ((2, 0, n),),
        ((1, 0, n), (3, 0, n)),
        ((2, 1, n), (1, 1, n), (3, 1, n)),
        ((4, 0, n),),
        ((6, 0, n),),
        ((5, 0, n), (7, 0, n)),
        ((4, 1, n), (6, 1, n)),
        ((5, 1, n), (7, 1, n)),
    )
    where = jnp.stack([core, par, position, vid]).astype(jnp.int32)
    mixed, stream_out, stats = project(
        where, (a_own, a_ret, x_own, x_ret), stream, pieces, places
    )
    other = swap(stats, "head")
    normed = normalize(where, mixed, stats, other, scale_mod, shift_mod)
    return (normed, stream_out)


def on_device(query, *rest):
    sizes = (lax.axis_size("video"), lax.axis_size("seq"), lax.axis_size("head"))
    if sizes == (2, 2 * HT, 2):
        return on_device_pair(query, *rest)
    return on_device_any(query, *rest)


def solution(mesh):
    return jax.shard_map(
        on_device,
        mesh=mesh,
        in_specs=(
            P(("video", "seq"), "head"),
            P(("video", "seq"), "head"),
            P(("video", "seq"), "head"),
            P(("video", "seq"), "head"),
            P("video"),
            P("video"),
            P("seq", "head"),
        ),
        out_specs=(P(("video", "seq"), "head"), P(("video", "seq"), "head")),
        check_vma=False,
    )
```

```python
import functools
import math

import jax
import jax.numpy as jnp
from jax import lax
from jax.experimental import pallas as pl
from jax.experimental.pallas import tpu as pltpu
from jax.sharding import PartitionSpec as P


D = 3072
HD = 128
TILE = 128
HT = 4
EPS = 1e-06
EXP2_SCALE = math.log2(math.e) / math.sqrt(HD)
AWAY = -1e30


def shifted(value, axis, steps):
    count = lax.axis_size(axis)
    leading, last = (max(0, -steps), min(count, count - steps))
    return lax.ppermute(value, axis, [(source, source + steps) for source in range(leading, last)])


def attend_tile(query_tile, keys_all, values_all, visible):
    tile_rows, features = query_tile.shape
    heads_here = features // HD

    def one_head(head):
        head_query = lax.dynamic_slice_in_dim(query_tile, head * HD, HD, 1)
        head_key = lax.dynamic_slice_in_dim(keys_all, head * HD, HD, 1)
        head_value = lax.dynamic_slice_in_dim(values_all, head * HD, HD, 1)
        scores = jnp.einsum(
            "nd,md->nm", head_query, head_key, preferred_element_type=jnp.float32
        ) / math.sqrt(HD)
        scores = jnp.where(visible[None, :], scores, -jnp.inf)
        top = jnp.max(scores, axis=1, keepdims=True)
        expo = jnp.exp(scores - top)
        total = jnp.sum(expo, axis=1, keepdims=True)
        probs = expo.astype(jnp.bfloat16)
        weighted = jnp.dot(probs, head_value, preferred_element_type=jnp.float32)
        return (weighted / total).astype(jnp.bfloat16)

    per_head = lax.map(one_head, jnp.arange(heads_here, dtype=jnp.int32))
    return jnp.transpose(per_head, (1, 0, 2)).reshape(tile_rows, features)


def on_device_any(query, key, value, stream, shift_mod, scale_mod, out_weight):
    slab_rows = query.shape[0]
    width_tiles = slab_rows // TILE
    layers = lax.axis_size("seq") // HT
    position = lax.axis_index("seq")
    time_tile = position // HT
    height_tile = position % HT
    key_value = jnp.stack([key, value])
    vertical = {0: key_value}
    for offset in (HT, -HT):
        vertical[-offset // HT] = shifted(key_value, "seq", offset)
    column = jnp.stack([vertical[-1], vertical[0], vertical[1]])
    sideways = {0: column}
    for offset in (1, -1):
        sideways[-offset] = shifted(column, "seq", offset)
    neighbours = []
    for across in (-1, 0, 1):
        for upward in (-1, 0, 1):
            inside = (time_tile + across >= 0) & (time_tile + across < layers)
            inside = inside & (height_tile + upward >= 0) & (height_tile + upward < HT)
            neighbours.append((sideways[upward][across + 1], inside))
    results = []
    for tile_pos in range(width_tiles):
        lowest = max(tile_pos - 1, 0)
        highest = min(tile_pos + 1, width_tiles - 1)
        begin = lowest * TILE
        count = (highest - lowest + 1) * TILE
        keys_here = jnp.concatenate(
            [paired[0][begin : begin + count] for paired, inside in neighbours], 0
        )
        values_here = jnp.concatenate(
            [paired[1][begin : begin + count] for paired, inside in neighbours], 0
        )
        flags = jnp.concatenate(
            [jnp.broadcast_to(inside, (count,)) for paired, inside in neighbours]
        )
        query_tile = query[tile_pos * TILE : (tile_pos + 1) * TILE]
        results.append(attend_tile(query_tile, keys_here, values_here, flags))
    attended = jnp.concatenate(results, 0)
    width_cols = D // lax.axis_size("head")
    first_col = lax.axis_index("head") * width_cols
    weight_cols = lax.all_gather(out_weight, "seq", axis=0, tiled=True)
    weight_rows = lax.all_to_all(weight_cols, "head", split_axis=0, concat_axis=1, tiled=True)
    partial_value = jnp.dot(attended, weight_rows, preferred_element_type=jnp.float32)
    share = lax.psum_scatter(partial_value, "head", scatter_dimension=1, tiled=True)
    mixed = stream.astype(jnp.float32) + share
    totals, squares = lax.psum((jnp.sum(mixed, axis=1), jnp.sum(mixed * mixed, axis=1)), "head")
    mean = (totals / D)[:, None]
    var = (squares / D)[:, None] - mean * mean
    scale_part = lax.dynamic_slice_in_dim(scale_mod, first_col, width_cols, 0)
    shift_part = lax.dynamic_slice_in_dim(shift_mod, first_col, width_cols, 0)
    normed = ((mixed - mean) * lax.rsqrt(var + EPS) * (1.0 + scale_part) + shift_part).astype(
        jnp.bfloat16
    )
    return (normed, mixed.astype(jnp.bfloat16))


def attention_kernel(info, query, own, y_own, z_own, e_kv, y_oth, k_far, v_far, out):
    rows = query.shape[0]
    tiles = rows // TILE
    away = jnp.where(info[1] == 1, jnp.float32(0), jnp.float32(AWAY))
    parts = [(ref.at[0], ref.at[1], False) for ref in (own, y_own, e_kv, y_oth)]
    parts += [(z_own.at[0], z_own.at[1], True), (k_far, v_far, True)]
    for tile in range(tiles):
        begin = max(tile - 1, 0) * TILE
        end = (min(tile + 1, tiles - 1) + 1) * TILE
        q = query[tile * TILE : (tile + 1) * TILE, :]
        scores = []
        tops = []
        for keys, values, far in parts:
            s = lax.dot_general(
                q,
                keys[begin:end, :],
                (((1,), (1,)), ((), ())),
                preferred_element_type=jnp.float32,
            )
            scores.append(s)
            top = jnp.max(s, axis=1, keepdims=True)
            tops.append(top + away if far else top)
        top = functools.reduce(jnp.maximum, tops)
        total = jnp.zeros((TILE, 1), jnp.float32)
        acc = jnp.zeros((TILE, HD), jnp.float32)
        for s, (keys, values, far) in zip(scores, parts):
            p = jnp.exp2((s - (top - away if far else top)) * EXP2_SCALE)
            total = total + jnp.sum(p, axis=1, keepdims=True)
            acc = acc + jnp.dot(
                p.astype(jnp.bfloat16), values[begin:end, :], preferred_element_type=jnp.float32
            )
        out[tile * TILE : (tile + 1) * TILE, :] = (acc / total).astype(jnp.bfloat16)


def attention(info, query, own, parts):
    rows = query.shape[0]
    cols = parts[0].shape[2]
    heads = cols // HD
    if own:
        q_map = lambda j, info: (0, info[0] * heads + j)
    else:
        q_map = lambda j, info: (0, j)
    pair_spec = pl.BlockSpec((2, rows, HD), lambda j, info: (0, 0, j))
    one_spec = pl.BlockSpec((rows, HD), lambda j, info: (0, j))
    pairs = rows * 7 * TILE * 2 * heads
    return pl.pallas_call(
        attention_kernel,
        grid_spec=pltpu.PrefetchScalarGridSpec(
            num_scalar_prefetch=1,
            grid=(heads,),
            in_specs=[pl.BlockSpec((rows, HD), q_map)] + [pair_spec] * 5 + [one_spec] * 2,
            out_specs=pl.BlockSpec((rows, HD), lambda j, info: (0, j)),
        ),
        out_shape=jax.ShapeDtypeStruct((rows, cols), jnp.bfloat16),
        compiler_params=pltpu.CompilerParams(vmem_limit_bytes=12 << 20),
        cost_estimate=pl.CostEstimate(
            flops=pairs * HD * 4, transcendentals=pairs, bytes_accessed=rows * cols * 28
        ),
        name="attend",
    )(info, query, *parts)


def project_kernel(
    info, a_own, a_ret, x_own, x_ret, stream_hbm, *rest, places, count
):
    pieces = rest[:count]
    mixed, stream_out, stats, weight, left, stream, sems = rest[count:]
    core, par, pos, vid = info[0], info[1], info[2], info[3]
    copies = []
    for piece, (flip, half, size) in zip(pieces, places):
        other = pos ^ flip
        if half is None:
            row = other * size
        else:
            row = other * (2 * size) + (vid if half == 0 else 1 - vid) * size
        copy = pltpu.make_async_copy(
            piece, weight.at[pl.ds(pl.multiple_of(row, 32), size)], sems.at[len(copies)]
        )
        copy.start()
        copies.append(copy)
    copy = pltpu.make_async_copy(stream_hbm, stream, sems.at[len(copies)])
    copy.start()
    copies.append(copy)
    cols = a_own.shape[1]
    for ref, block in (
        (a_own, core * 2 + par),
        (a_ret, core * 2 + 1 - par),
        (x_own, (1 - core) * 2 + par),
        (x_ret, (1 - core) * 2 + 1 - par),
    ):
        left[:, pl.ds(pl.multiple_of(block * cols, HD), cols)] = ref[...]
    for copy in copies:
        copy.wait()
    rows, width = stream.shape
    step = 512
    total = jnp.zeros((rows, 1), jnp.float32)
    for first in range(0, width, step):
        got = jnp.dot(
            left[...], weight[:, first : first + step], preferred_element_type=jnp.float32
        ) + stream[:, first : first + step].astype(jnp.float32)
        mixed[:, first : first + step] = got
        stream_out[:, first : first + step] = got.astype(jnp.bfloat16)
        total = total + jnp.sum(got, axis=1, keepdims=True)
    mean = total * (1.0 / width)
    square = jnp.zeros((rows, 1), jnp.float32)
    for first in range(0, width, step):
        off = mixed[:, first : first + step] - mean
        square = square + jnp.sum(off * off, axis=1, keepdims=True)
    lane = lax.broadcasted_iota(jnp.int32, stats.shape, 1)
    stats[...] = jnp.where(lane == 0, mean, square)


def project(info, blocks, stream, pieces, places):
    rows, width = stream.shape
    depth = 4 * blocks[0].shape[1]
    copies = len(places)
    vmem = pl.BlockSpec(memory_space=pltpu.VMEM)
    return pl.pallas_call(
        functools.partial(project_kernel, places=places, count=len(pieces)),
        in_specs=[pl.BlockSpec(memory_space=pltpu.SMEM)]
        + [vmem] * 4
        + [pl.BlockSpec(memory_space=pltpu.HBM)] * (1 + len(pieces)),
        out_specs=[vmem] * 3,
        out_shape=[
            jax.ShapeDtypeStruct((rows, width), jnp.float32),
            jax.ShapeDtypeStruct((rows, width), jnp.bfloat16),
            jax.ShapeDtypeStruct((rows, HD), jnp.float32),
        ],
        scratch_shapes=[
            pltpu.VMEM((depth, width), jnp.bfloat16),
            pltpu.VMEM((rows, depth), jnp.bfloat16),
            pltpu.VMEM((rows, width), jnp.bfloat16),
            pltpu.SemaphoreType.DMA((copies + 1,)),
        ],
        compiler_params=pltpu.CompilerParams(vmem_limit_bytes=20 << 20),
        cost_estimate=pl.CostEstimate(
            flops=2 * rows * depth * width,
            transcendentals=0,
            bytes_accessed=depth * width * 2 + rows * width * 8,
        ),
        name="project",
    )(info, *blocks, stream, *pieces)


def norm_kernel(info, mixed, mine, other, scale, shift, out, *, half):
    m0, m1 = mine[:, 0:1], other[:, 0:1]
    q0, q1 = mine[:, 1:2], other[:, 1:2]
    mean = 0.5 * (m0 + m1)
    gap = m0 - m1
    var = (q0 + q1 + gap * gap * (0.5 * half)) * (0.5 / half)
    rate = lax.rsqrt(var + EPS)
    out[...] = ((mixed[...] - mean) * rate * (1.0 + scale[...]) + shift[...]).astype(jnp.bfloat16)


def normalize(info, mixed, mine, other, scale_mod, shift_mod):
    rows, width = mixed.shape
    step = TILE
    row_block = pl.BlockSpec((step, width), lambda i, info: (i, 0))
    stat_block = pl.BlockSpec((step, HD), lambda i, info: (i, 0))
    mod_block = pl.BlockSpec((1, width), lambda i, info: (0, info[0]))
    return pl.pallas_call(
        functools.partial(norm_kernel, half=float(width)),
        grid_spec=pltpu.PrefetchScalarGridSpec(
            num_scalar_prefetch=1,
            grid=(rows // step,),
            in_specs=[row_block, stat_block, stat_block, mod_block, mod_block],
            out_specs=row_block,
        ),
        out_shape=jax.ShapeDtypeStruct((rows, width), jnp.bfloat16),
        compiler_params=pltpu.CompilerParams(vmem_limit_bytes=12 << 20),
        cost_estimate=pl.CostEstimate(
            flops=6 * rows * width, transcendentals=rows, bytes_accessed=rows * width * 6
        ),
        name="normalize",
    )(info, mixed, mine, other, scale_mod[None, :], shift_mod[None, :])


def after(value, *done):
    return lax.optimization_barrier((value,) + done)[0]


def on_device_pair(query, key, value, stream, shift_mod, scale_mod, out_weight):
    count = lax.axis_size("seq")
    position = lax.axis_index("seq")
    core = lax.axis_index("head")
    vid = lax.axis_index("video")
    par = position // HT
    height = position % HT
    relayed = jnp.where((height == 1) | (height == 2), 1, 0)
    half_cols = query.shape[1] // 2

    def flip(x, mask):
        return lax.ppermute(x, "seq", [(i, i ^ mask) for i in range(count)])

    def swap(x, axis):
        return lax.ppermute(x, axis, [(0, 1), (1, 0)])

    def some(x, mask, sources):
        pairs = [(i, i ^ mask) for i in range(count) if i % HT in sources]
        return lax.ppermute(x, "seq", pairs)

    def heads(x, which):
        return lax.dynamic_slice_in_dim(x, which * half_cols, half_cols, 1)

    give = jnp.stack([heads(key, 1 - par), heads(value, 1 - par)])
    give_q = heads(query, 1 - par)
    own = jnp.stack([heads(key, par), heads(value, par)])
    rows_half = out_weight.shape[0] // 2
    w_own = lax.dynamic_slice_in_dim(out_weight, vid * rows_half, rows_half, 0)

    e_kv = flip(give, HT)
    y_own = flip(own, 1)
    w_z1 = flip(w_own, 2)
    z_own = some(y_own, 2, (0, 3))
    w_ya = flip(after(w_own, y_own), 1)
    w_yb = flip(after(w_z1, y_own), 1)
    w_xa = swap(w_z1, "video")
    w_t = flip(after(w_own, e_kv), HT)
    y_oth = flip(e_kv, 1)
    v_z = some(e_kv[1], 2, (1, 2))
    w_xb = swap(w_ya, "video")
    w_xc = swap(w_yb, "video")
    e_q = flip(after(give_q, w_t), HT)
    k_far = some(y_oth[0], 2, (0, 3))
    v_far = some(v_z, 1, (0, 3))
    w_yc = flip(w_t, 1)
    w_z2 = flip(w_t, 2)
    w_xd = swap(w_t, "video")
    w_yd = flip(w_z2, 1)
    w_xe = swap(w_z2, "video")
    w_xf = swap(w_yc, "video")
    w_xg = swap(w_yd, "video")

    info = jnp.stack([par, relayed]).astype(jnp.int32)
    parts = (own, y_own, z_own, e_kv, y_oth, k_far, v_far)
    out_other = attention(info, e_q, False, parts)
    a_ret = flip(out_other, HT)
    a_own = attention(info, query, True, parts)
    x_own = swap(a_own, "head")
    x_ret = swap(a_ret, "head")

    n = rows_half
    here = (w_z1, w_ya, w_yb, w_t, w_z2, w_yc, w_yd)
    across = (w_xa, w_xb, w_xc, w_xd, w_xe, w_xf, w_xg)
    flips = (2, 1, 3, 4, 6, 5, 7)
    pieces = (out_weight,) + here + across
    places = ((0, None, 2 * n),)
    places += tuple((mask, half, n) for half in (0, 1) for mask in flips)
    where = jnp.stack([core, par, position, vid]).astype(jnp.int32)
    mixed, stream_out, stats = project(
        where, (a_own, a_ret, x_own, x_ret), stream, pieces, places
    )
    other = swap(stats, "head")
    normed = normalize(where, mixed, stats, other, scale_mod, shift_mod)
    return (normed, stream_out)


PAIR = {"video": 2, "seq": 2 * HT, "head": 2}


def on_device(query, *rest):
    sizes = {axis: lax.axis_size(axis) for axis in PAIR}
    if sizes == PAIR:
        return on_device_pair(query, *rest)
    return on_device_any(query, *rest)


def solution(mesh):
    return jax.shard_map(
        on_device,
        mesh=mesh,
        in_specs=(
            P(("video", "seq"), "head"),
            P(("video", "seq"), "head"),
            P(("video", "seq"), "head"),
            P(("video", "seq"), "head"),
            P("video"),
            P("video"),
            P("seq", "head"),
        ),
        out_specs=(P(("video", "seq"), "head"), P(("video", "seq"), "head")),
        check_vma=False,
    )
```

```python
import functools
import itertools
import math

import jax
import jax.numpy as jnp
from jax import lax
from jax.experimental import pallas as pl
from jax.experimental.pallas import tpu as pltpu
from jax.sharding import PartitionSpec as P


D = 3072
HD = 128
TILE = 128
HT = 4
EPS = 1e-06
EXP2_SCALE = math.log2(math.e) / math.sqrt(HD)
AWAY = -1e30
GROUP = 3


def shifted(value, axis, steps):
    count = lax.axis_size(axis)
    leading, last = (max(0, -steps), min(count, count - steps))
    return lax.ppermute(value, axis, [(source, source + steps) for source in range(leading, last)])


def attend_tile(query_tile, keys_all, values_all, visible):
    tile_rows, features = query_tile.shape
    heads_here = features // HD

    def one_head(head):
        head_query = lax.dynamic_slice_in_dim(query_tile, head * HD, HD, 1)
        head_key = lax.dynamic_slice_in_dim(keys_all, head * HD, HD, 1)
        head_value = lax.dynamic_slice_in_dim(values_all, head * HD, HD, 1)
        scores = jnp.einsum(
            "nd,md->nm", head_query, head_key, preferred_element_type=jnp.float32
        ) / math.sqrt(HD)
        scores = jnp.where(visible[None, :], scores, -jnp.inf)
        top = jnp.max(scores, axis=1, keepdims=True)
        expo = jnp.exp(scores - top)
        total = jnp.sum(expo, axis=1, keepdims=True)
        probs = expo.astype(jnp.bfloat16)
        weighted = jnp.dot(probs, head_value, preferred_element_type=jnp.float32)
        return (weighted / total).astype(jnp.bfloat16)

    per_head = lax.map(one_head, jnp.arange(heads_here, dtype=jnp.int32))
    return jnp.transpose(per_head, (1, 0, 2)).reshape(tile_rows, features)


def on_device_any(query, key, value, stream, shift_mod, scale_mod, out_weight):
    slab_rows = query.shape[0]
    width_tiles = slab_rows // TILE
    layers = lax.axis_size("seq") // HT
    position = lax.axis_index("seq")
    time_tile = position // HT
    height_tile = position % HT
    key_value = jnp.stack([key, value])
    vertical = {0: key_value}
    for offset in (HT, -HT):
        vertical[-offset // HT] = shifted(key_value, "seq", offset)
    column = jnp.stack([vertical[-1], vertical[0], vertical[1]])
    sideways = {0: column}
    for offset in (1, -1):
        sideways[-offset] = shifted(column, "seq", offset)
    neighbours = []
    for across in (-1, 0, 1):
        for upward in (-1, 0, 1):
            inside = (time_tile + across >= 0) & (time_tile + across < layers)
            inside = inside & (height_tile + upward >= 0) & (height_tile + upward < HT)
            neighbours.append((sideways[upward][across + 1], inside))
    results = []
    for tile_pos in range(width_tiles):
        lowest = max(tile_pos - 1, 0)
        highest = min(tile_pos + 1, width_tiles - 1)
        begin = lowest * TILE
        count = (highest - lowest + 1) * TILE
        keys_here = jnp.concatenate(
            [paired[0][begin : begin + count] for paired, inside in neighbours], 0
        )
        values_here = jnp.concatenate(
            [paired[1][begin : begin + count] for paired, inside in neighbours], 0
        )
        flags = jnp.concatenate(
            [jnp.broadcast_to(inside, (count,)) for paired, inside in neighbours]
        )
        query_tile = query[tile_pos * TILE : (tile_pos + 1) * TILE]
        results.append(attend_tile(query_tile, keys_here, values_here, flags))
    attended = jnp.concatenate(results, 0)
    width_cols = D // lax.axis_size("head")
    first_col = lax.axis_index("head") * width_cols
    weight_cols = lax.all_gather(out_weight, "seq", axis=0, tiled=True)
    weight_rows = lax.all_to_all(weight_cols, "head", split_axis=0, concat_axis=1, tiled=True)
    partial_value = jnp.dot(attended, weight_rows, preferred_element_type=jnp.float32)
    share = lax.psum_scatter(partial_value, "head", scatter_dimension=1, tiled=True)
    mixed = stream.astype(jnp.float32) + share
    totals, squares = lax.psum((jnp.sum(mixed, axis=1), jnp.sum(mixed * mixed, axis=1)), "head")
    mean = (totals / D)[:, None]
    var = (squares / D)[:, None] - mean * mean
    scale_part = lax.dynamic_slice_in_dim(scale_mod, first_col, width_cols, 0)
    shift_part = lax.dynamic_slice_in_dim(shift_mod, first_col, width_cols, 0)
    normed = ((mixed - mean) * lax.rsqrt(var + EPS) * (1.0 + scale_part) + shift_part).astype(
        jnp.bfloat16
    )
    return (normed, mixed.astype(jnp.bfloat16))


def lane_blocks(x, op):
    return functools.reduce(op, [x[:, c : c + HD] for c in range(0, x.shape[1], HD)])


def attention_kernel(info, query, *refs, kinds, own, resume, final):
    refs = list(refs)
    parts = []
    for stacked, far in kinds:
        if stacked:
            ref = refs.pop(0)
            parts.append((ref.at[0], ref.at[1], far))
        else:
            parts.append((refs.pop(0), refs.pop(0), far))
    before = [refs.pop(0) for _ in range(3)] if resume else None
    rows = query.shape[0]
    tiles = rows // TILE
    heads = refs[0].shape[1] // HD
    away = jnp.where(info[1] == 1, jnp.float32(0), jnp.float32(AWAY))
    units = list(itertools.product(range(heads), range(tiles)))

    def place(head, tile):
        begin = max(tile - 1, 0) * TILE
        end = (min(tile + 1, tiles - 1) + 1) * TILE
        here = slice(tile * TILE, (tile + 1) * TILE)
        return here, slice(begin, end), slice(head * HD, (head + 1) * HD)

    def score(head, tile):
        here, seen, feats = place(head, tile)
        if own:
            q = query[here, pl.ds(pl.multiple_of((info[0] * heads + head) * HD, HD), HD)]
        else:
            q = query[here, feats]
        return [
            lax.dot_general(
                q,
                keys[seen, feats],
                (((1,), (1,)), ((), ())),
                preferred_element_type=jnp.float32,
            )
            for keys, _, _ in parts
        ]

    def highest(scores):
        tops = [
            lane_blocks(s, jnp.maximum) + (away if far else 0.0)
            for s, (_, _, far) in zip(scores, parts)
        ]
        return jnp.max(functools.reduce(jnp.maximum, tops), axis=1, keepdims=True)

    def gather(head, tile, scores, top):
        here, seen, feats = place(head, tile)
        acc = jnp.zeros((TILE, HD), jnp.float32)
        total = jnp.zeros((TILE, HD), jnp.float32)
        if resume:
            old = before[2][here, feats][:, 0:1]
            top = jnp.maximum(top, old)
            keep = jnp.exp2((old - top) * EXP2_SCALE)
            acc = before[0][here, feats] * keep
        for s, (_, values, far) in zip(scores, parts):
            p = jnp.exp2((s - (top - away if far else top)) * EXP2_SCALE)
            total = total + lane_blocks(p, jnp.add)
            acc = acc + jnp.dot(
                p.astype(jnp.bfloat16), values[seen, feats], preferred_element_type=jnp.float32
            )
        total = jnp.sum(total, axis=1, keepdims=True)
        if resume:
            total = total + before[1][here, feats][:, 0:1] * keep
        return acc, total, top

    def write(head, tile, acc, total, top):
        here, _, feats = place(head, tile)
        if final:
            refs[0][here, feats] = (acc / total).astype(jnp.bfloat16)
        else:
            refs[0][here, feats] = acc
            refs[1][here, feats] = jnp.broadcast_to(total, (TILE, HD))
            refs[2][here, feats] = jnp.broadcast_to(top, (TILE, HD))

    for first in range(0, len(units), GROUP):
        group = units[first : first + GROUP]
        scores = [score(*unit) for unit in group]
        tops = [highest(s) for s in scores]
        done = [gather(*unit, s, top) for unit, s, top in zip(group, scores, tops)]
        for unit, result in zip(group, done):
            write(*unit, *result)


def attention(info, query, own, parts, before=(), final=True):
    rows = query.shape[0]
    cols = parts[0][0][0].shape[-1]
    heads = cols // HD
    vmem = pl.BlockSpec(memory_space=pltpu.VMEM)
    operands = [x for given, far in parts for x in given] + list(before)
    kinds = tuple((len(given) == 1, far) for given, far in parts)
    pairs = rows * 7 * TILE * len(parts) * heads // 3
    if final:
        out_shape = jax.ShapeDtypeStruct((rows, cols), jnp.bfloat16)
        out_specs = vmem
    else:
        out_shape = [jax.ShapeDtypeStruct((rows, cols), jnp.float32)] * 3
        out_specs = [vmem] * 3
    return pl.pallas_call(
        functools.partial(
            attention_kernel, kinds=kinds, own=own, resume=bool(before), final=final
        ),
        in_specs=[pl.BlockSpec(memory_space=pltpu.SMEM)] + [vmem] * (1 + len(operands)),
        out_specs=out_specs,
        out_shape=out_shape,
        compiler_params=pltpu.CompilerParams(vmem_limit_bytes=12 << 20),
        cost_estimate=pl.CostEstimate(
            flops=pairs * HD * 4, transcendentals=pairs, bytes_accessed=rows * cols * 4 * len(parts)
        ),
        name="attend",
    )(info, query, *operands)


def project_kernel(info, a_own, a_ret, x_own, x_ret, stream, *rest, places):
    pieces = rest[: len(places)]
    mixed, stream_out, stats, weight, left = rest[len(places) :]
    core, par, pos, vid = info[0], info[1], info[2], info[3]
    cols = a_own.shape[1]
    for ref, block in (
        (a_own, core * 2 + par),
        (a_ret, core * 2 + 1 - par),
        (x_own, (1 - core) * 2 + par),
        (x_ret, (1 - core) * 2 + 1 - par),
    ):
        left[:, pl.ds(pl.multiple_of(block * cols, HD), cols)] = ref[...]
    for piece, (flip, half, size) in zip(pieces, places):
        row = (pos ^ flip) * size
        if half is not None:
            row = row * 2 + (vid if half == 0 else 1 - vid) * size
        weight[pl.ds(pl.multiple_of(row, 32), size), :] = piece[...]
    rows, width = stream.shape
    step = width // 3
    total = jnp.zeros((rows, HD), jnp.float32)
    for first in range(0, width, step):
        block = slice(first, first + step)
        got = jnp.dot(
            left[...], weight[:, block], preferred_element_type=jnp.float32
        ) + stream[:, block].astype(jnp.float32)
        mixed[:, block] = got
        stream_out[:, block] = got.astype(jnp.bfloat16)
        total = total + lane_blocks(got, jnp.add)
    mean = jnp.sum(total, axis=1, keepdims=True) * (1.0 / width)
    square = jnp.zeros((rows, HD), jnp.float32)
    for first in range(0, width, HD):
        off = mixed[:, first : first + HD] - mean
        square = square + off * off
    square = jnp.sum(square, axis=1, keepdims=True)
    lane = lax.broadcasted_iota(jnp.int32, stats.shape, 1)
    stats[...] = jnp.where(lane == 0, mean, square)


def project(info, blocks, stream, pieces, places):
    rows, width = stream.shape
    depth = 4 * blocks[0].shape[1]
    vmem = pl.BlockSpec(memory_space=pltpu.VMEM)
    return pl.pallas_call(
        functools.partial(project_kernel, places=places),
        in_specs=[pl.BlockSpec(memory_space=pltpu.SMEM)] + [vmem] * (5 + len(pieces)),
        out_specs=[vmem] * 3,
        out_shape=[
            jax.ShapeDtypeStruct((rows, width), jnp.float32),
            jax.ShapeDtypeStruct((rows, width), jnp.bfloat16),
            jax.ShapeDtypeStruct((rows, HD), jnp.float32),
        ],
        scratch_shapes=[
            pltpu.VMEM((depth, width), jnp.bfloat16),
            pltpu.VMEM((rows, depth), jnp.bfloat16),
        ],
        compiler_params=pltpu.CompilerParams(vmem_limit_bytes=24 << 20),
        cost_estimate=pl.CostEstimate(
            flops=2 * rows * depth * width,
            transcendentals=0,
            bytes_accessed=depth * width * 2 + rows * width * 8,
        ),
        name="project",
    )(info, *blocks, stream, *pieces)


def norm_kernel(info, mixed, mine, other, scale, shift, out, held, sems):
    rows, width = mixed.shape
    step = rows // sems.shape[0]
    m0, m1 = mine[:, 0:1], other[:, 0:1]
    q0, q1 = mine[:, 1:2], other[:, 1:2]
    mean = 0.5 * (m0 + m1)
    gap = m0 - m1
    var = (q0 + q1 + gap * gap * (0.5 * width)) * (0.5 / width)
    rate = lax.rsqrt(var + EPS)
    columns = pl.ds(pl.multiple_of(info[0] * width, HD), width)
    gain = 1.0 + scale[:, columns]
    bias = shift[:, columns]
    copies = []
    for first in range(0, rows, step):
        here = slice(first, first + step)
        held[here, :] = ((mixed[here, :] - mean[here]) * rate[here] * gain + bias).astype(
            jnp.bfloat16
        )
        copies.append(
            pltpu.make_async_copy(held.at[here, :], out.at[here, :], sems.at[len(copies)])
        )
        copies[-1].start()
    for copy in copies:
        copy.wait()


def normalize(info, mixed, mine, other, scale_mod, shift_mod):
    rows, width = mixed.shape
    vmem = pl.BlockSpec(memory_space=pltpu.VMEM)
    return pl.pallas_call(
        norm_kernel,
        in_specs=[pl.BlockSpec(memory_space=pltpu.SMEM)] + [vmem] * 5,
        out_specs=pl.BlockSpec(memory_space=pltpu.HBM),
        out_shape=jax.ShapeDtypeStruct((rows, width), jnp.bfloat16),
        scratch_shapes=[
            pltpu.VMEM((rows, width), jnp.bfloat16),
            pltpu.SemaphoreType.DMA((rows // TILE,)),
        ],
        compiler_params=pltpu.CompilerParams(vmem_limit_bytes=12 << 20),
        cost_estimate=pl.CostEstimate(
            flops=6 * rows * width, transcendentals=rows, bytes_accessed=rows * width * 6
        ),
        name="normalize",
    )(info, mixed, mine, other, scale_mod[None, :], shift_mod[None, :])


def after(value, *done):
    return lax.optimization_barrier((value,) + done)[0]


def on_device_pair(query, key, value, stream, shift_mod, scale_mod, out_weight):
    count = lax.axis_size("seq")
    position = lax.axis_index("seq")
    core = lax.axis_index("head")
    vid = lax.axis_index("video")
    par = position // HT
    height = position % HT
    relayed = jnp.where((height == 1) | (height == 2), 1, 0)
    half_cols = query.shape[1] // 2

    def flip(x, mask):
        return lax.ppermute(x, "seq", [(i, i ^ mask) for i in range(count)])

    def swap(x, axis):
        return lax.ppermute(x, axis, [(0, 1), (1, 0)])

    def some(x, mask, sources):
        pairs = [(i, i ^ mask) for i in range(count) if i % HT in sources]
        return lax.ppermute(x, "seq", pairs)

    def heads(x, which):
        return lax.dynamic_slice_in_dim(x, which * half_cols, half_cols, 1)

    give_k = heads(key, 1 - par)
    own_k = heads(key, par)
    own_v = heads(value, par)
    give_v = heads(value, 1 - par)
    give_q = heads(query, 1 - par)
    rows_half = out_weight.shape[0] // 2
    w_own = lax.dynamic_slice_in_dim(out_weight, vid * rows_half, rows_half, 0)

    e_k = flip(give_k, HT)
    y_ok = flip(own_k, 1)
    w_z1 = flip(w_own, 2)
    e_v = flip(give_v, HT)
    y_ov = flip(own_v, 1)
    ov_z = some(own_v, 2, (1, 2))
    ok_far = some(y_ok, 2, (0, 3))
    w_ya = flip(after(w_own, y_ov), 1)
    ov_far = some(ov_z, 1, (0, 3))
    y_k = flip(e_k, 1)
    w_xa = swap(w_z1, "video")
    w_t = flip(after(w_own, e_v), HT)
    y_v = flip(e_v, 1)
    v_z = some(e_v, 2, (1, 2))
    k_far = some(y_k, 2, (0, 3))
    v_far = some(v_z, 1, (0, 3))
    w_xb = swap(w_ya, "video")
    w_yb = flip(after(w_z1, y_v), 1)
    w_xc = swap(w_yb, "video")
    w_z2 = flip(w_t, 2)
    e_q = flip(after(give_q, w_t), HT)
    w_xd = swap(w_t, "video")
    w_yc = flip(w_t, 1)
    w_yd = flip(w_z2, 1)
    w_xe = flip(w_xd, 2)
    w_xf = swap(w_yc, "video")
    w_xg = flip(w_xe, 1)

    info = jnp.stack([par, relayed]).astype(jnp.int32)
    parts = (
        ((own_k, own_v), False),
        ((y_ok, y_ov), False),
        ((ok_far, ov_far), True),
        ((e_k, e_v), False),
        ((y_k, y_v), False),
        ((k_far, v_far), True),
    )
    out_other = attention(info, e_q, False, parts)
    a_ret = flip(out_other, HT)
    a_own = attention(info, query, True, parts)
    x_own = swap(a_own, "head")
    x_ret = swap(a_ret, "head")

    n = rows_half
    here = (w_z1, w_ya, w_yb, w_t, w_z2, w_yc, w_yd)
    across = (w_xa, w_xb, w_xc, w_xd, w_xe, w_xf, w_xg)
    flips = (2, 1, 3, 4, 6, 5, 7)
    pieces = (out_weight,) + here + across
    places = ((0, None, 2 * n),)
    places += tuple((mask, half, n) for half in (0, 1) for mask in flips)
    where = jnp.stack([core, par, position, vid]).astype(jnp.int32)
    mixed, stream_out, stats = project(
        where, (a_own, a_ret, x_own, x_ret), stream, pieces, places
    )
    other = swap(stats, "head")
    normed = normalize(where, mixed, stats, other, scale_mod, shift_mod)
    return (normed, stream_out)


PAIR = {"video": 2, "seq": 2 * HT, "head": 2}


def on_device(query, *rest):
    sizes = {axis: lax.axis_size(axis) for axis in PAIR}
    if sizes == PAIR:
        return on_device_pair(query, *rest)
    return on_device_any(query, *rest)


def solution(mesh):
    return jax.shard_map(
        on_device,
        mesh=mesh,
        in_specs=(
            P(("video", "seq"), "head"),
            P(("video", "seq"), "head"),
            P(("video", "seq"), "head"),
            P(("video", "seq"), "head"),
            P("video"),
            P("video"),
            P("seq", "head"),
        ),
        out_specs=(P(("video", "seq"), "head"), P(("video", "seq"), "head")),
        check_vma=False,
    )
```

```python
import functools
import itertools
import math

import jax
import jax.numpy as jnp
from jax import lax
from jax.experimental import pallas as pl
from jax.experimental.pallas import tpu as pltpu
from jax.sharding import PartitionSpec as P


D = 3072
HD = 128
TILE = 128
HT = 4
EPS = 1e-06
EXP2_SCALE = math.log2(math.e) / math.sqrt(HD)
AWAY = -1e30
GROUP = 3


def shifted(value, axis, steps):
    count = lax.axis_size(axis)
    leading, last = (max(0, -steps), min(count, count - steps))
    return lax.ppermute(value, axis, [(source, source + steps) for source in range(leading, last)])


def attend_tile(query_tile, keys_all, values_all, visible):
    tile_rows, features = query_tile.shape
    heads_here = features // HD

    def one_head(head):
        head_query = lax.dynamic_slice_in_dim(query_tile, head * HD, HD, 1)
        head_key = lax.dynamic_slice_in_dim(keys_all, head * HD, HD, 1)
        head_value = lax.dynamic_slice_in_dim(values_all, head * HD, HD, 1)
        scores = jnp.einsum(
            "nd,md->nm", head_query, head_key, preferred_element_type=jnp.float32
        ) / math.sqrt(HD)
        scores = jnp.where(visible[None, :], scores, -jnp.inf)
        top = jnp.max(scores, axis=1, keepdims=True)
        expo = jnp.exp(scores - top)
        total = jnp.sum(expo, axis=1, keepdims=True)
        probs = expo.astype(jnp.bfloat16)
        weighted = jnp.dot(probs, head_value, preferred_element_type=jnp.float32)
        return (weighted / total).astype(jnp.bfloat16)

    per_head = lax.map(one_head, jnp.arange(heads_here, dtype=jnp.int32))
    return jnp.transpose(per_head, (1, 0, 2)).reshape(tile_rows, features)


def on_device_any(query, key, value, stream, shift_mod, scale_mod, out_weight):
    slab_rows = query.shape[0]
    width_tiles = slab_rows // TILE
    layers = lax.axis_size("seq") // HT
    position = lax.axis_index("seq")
    time_tile = position // HT
    height_tile = position % HT
    key_value = jnp.stack([key, value])
    vertical = {0: key_value}
    for offset in (HT, -HT):
        vertical[-offset // HT] = shifted(key_value, "seq", offset)
    column = jnp.stack([vertical[-1], vertical[0], vertical[1]])
    sideways = {0: column}
    for offset in (1, -1):
        sideways[-offset] = shifted(column, "seq", offset)
    neighbours = []
    for across in (-1, 0, 1):
        for upward in (-1, 0, 1):
            inside = (time_tile + across >= 0) & (time_tile + across < layers)
            inside = inside & (height_tile + upward >= 0) & (height_tile + upward < HT)
            neighbours.append((sideways[upward][across + 1], inside))
    results = []
    for tile_pos in range(width_tiles):
        lowest = max(tile_pos - 1, 0)
        highest = min(tile_pos + 1, width_tiles - 1)
        begin = lowest * TILE
        count = (highest - lowest + 1) * TILE
        keys_here = jnp.concatenate(
            [paired[0][begin : begin + count] for paired, inside in neighbours], 0
        )
        values_here = jnp.concatenate(
            [paired[1][begin : begin + count] for paired, inside in neighbours], 0
        )
        flags = jnp.concatenate(
            [jnp.broadcast_to(inside, (count,)) for paired, inside in neighbours]
        )
        query_tile = query[tile_pos * TILE : (tile_pos + 1) * TILE]
        results.append(attend_tile(query_tile, keys_here, values_here, flags))
    attended = jnp.concatenate(results, 0)
    width_cols = D // lax.axis_size("head")
    first_col = lax.axis_index("head") * width_cols
    weight_cols = lax.all_gather(out_weight, "seq", axis=0, tiled=True)
    weight_rows = lax.all_to_all(weight_cols, "head", split_axis=0, concat_axis=1, tiled=True)
    partial_value = jnp.dot(attended, weight_rows, preferred_element_type=jnp.float32)
    share = lax.psum_scatter(partial_value, "head", scatter_dimension=1, tiled=True)
    mixed = stream.astype(jnp.float32) + share
    totals, squares = lax.psum((jnp.sum(mixed, axis=1), jnp.sum(mixed * mixed, axis=1)), "head")
    mean = (totals / D)[:, None]
    var = (squares / D)[:, None] - mean * mean
    scale_part = lax.dynamic_slice_in_dim(scale_mod, first_col, width_cols, 0)
    shift_part = lax.dynamic_slice_in_dim(shift_mod, first_col, width_cols, 0)
    normed = ((mixed - mean) * lax.rsqrt(var + EPS) * (1.0 + scale_part) + shift_part).astype(
        jnp.bfloat16
    )
    return (normed, mixed.astype(jnp.bfloat16))


def lane_blocks(x, op):
    return functools.reduce(op, [x[:, c : c + HD] for c in range(0, x.shape[1], HD)])


def attention_kernel(info, query, *refs, returned):
    out, logs = refs[6:]
    parts = tuple((refs[i], refs[i + 1], i == 4) for i in (0, 2, 4))
    rows = query.shape[0]
    tiles = rows // TILE
    heads = out.shape[1] // HD
    away = jnp.where(info[1] == 1, jnp.float32(0), jnp.float32(AWAY))
    lane = lax.broadcasted_iota(jnp.int32, (TILE, HD), 1)
    log_of = [jnp.zeros((TILE, HD), jnp.float32) for _ in range(tiles)]

    def place(head, tile):
        begin = max(tile - 1, 0) * TILE
        end = (min(tile + 1, tiles - 1) + 1) * TILE
        here = slice(tile * TILE, (tile + 1) * TILE)
        return here, slice(begin, end), slice(head * HD, (head + 1) * HD)

    def score(head, tile):
        here, seen, feats = place(head, tile)
        return [
            lax.dot_general(
                query[here, feats],
                keys[seen, feats],
                (((1,), (1,)), ((), ())),
                preferred_element_type=jnp.float32,
            )
            for keys, _, _ in parts
        ]

    def highest(scores):
        tops = [
            lane_blocks(s, jnp.maximum) + (away if far else 0.0)
            for s, (_, _, far) in zip(scores, parts)
        ]
        return jnp.max(functools.reduce(jnp.maximum, tops), axis=1, keepdims=True)

    def gather(head, tile, scores, top):
        _, seen, feats = place(head, tile)
        acc = jnp.zeros((TILE, HD), jnp.float32)
        total = jnp.zeros((TILE, HD), jnp.float32)
        for s, (_, values, far) in zip(scores, parts):
            p = jnp.exp2((s - (top - away if far else top)) * EXP2_SCALE)
            total = total + lane_blocks(p, jnp.add)
            acc = acc + jnp.dot(
                p.astype(jnp.bfloat16), values[seen, feats], preferred_element_type=jnp.float32
            )
        return acc, jnp.sum(total, axis=1, keepdims=True)

    units = list(itertools.product(range(heads), range(tiles)))
    for start in range(0, len(units), GROUP):
        group = units[start : start + GROUP]
        scores = [score(*unit) for unit in group]
        tops = [highest(s) for s in scores]
        done = [gather(*unit, s, top) for unit, s, top in zip(group, scores, tops)]
        for (head, tile), top, (acc, total) in zip(group, tops, done):
            here, _, feats = place(head, tile)
            out[here, feats] = (acc / total).astype(out.dtype)
            log = top * EXP2_SCALE + jnp.log2(total)
            log_of[tile] = jnp.where(lane == head, log, log_of[tile])
    for tile in range(tiles):
        here = slice(tile * TILE, (tile + 1) * TILE)
        if returned:
            logs[:, here] = jnp.transpose(log_of[tile])[: logs.shape[0], :]
        else:
            logs[here, :] = log_of[tile]


def attention(info, query, parts, returned):
    rows, cols = query.shape
    vmem = pl.BlockSpec(memory_space=pltpu.VMEM)
    pairs = rows * 7 * TILE * cols // HD
    if returned:
        kind, log_shape = jnp.bfloat16, (8, rows)
    else:
        kind, log_shape = jnp.float32, (rows, HD)
    return pl.pallas_call(
        functools.partial(attention_kernel, returned=returned),
        in_specs=[pl.BlockSpec(memory_space=pltpu.SMEM)] + [vmem] * (1 + len(parts)),
        out_specs=[vmem] * 2,
        out_shape=[
            jax.ShapeDtypeStruct((rows, cols), kind),
            jax.ShapeDtypeStruct(log_shape, jnp.float32),
        ],
        compiler_params=pltpu.CompilerParams(vmem_limit_bytes=12 << 20),
        cost_estimate=pl.CostEstimate(
            flops=pairs * HD * 4, transcendentals=pairs, bytes_accessed=rows * cols * 16
        ),
        name="attend",
    )(info, query, *parts)


def merge_kernel(mine, my_logs, got, got_logs, out):
    rows, cols = out.shape
    heads = cols // HD
    for tile in range(rows // TILE):
        here = slice(tile * TILE, (tile + 1) * TILE)
        fill = jnp.zeros((HD - got_logs.shape[0], TILE), jnp.float32)
        other = jnp.transpose(jnp.concatenate([got_logs[:, here], fill], 0))
        logs = my_logs[here, :]
        for head in range(heads):
            feats = slice(head * HD, (head + 1) * HD)
            gap = other[:, head : head + 1] - logs[:, head : head + 1]
            share = 1.0 / (1.0 + jnp.exp2(gap))
            far = got[here, feats].astype(jnp.float32)
            out[here, feats] = (mine[here, feats] * share + far * (1.0 - share)).astype(out.dtype)


def merge(mine, my_logs, got, got_logs):
    vmem = pl.BlockSpec(memory_space=pltpu.VMEM)
    return pl.pallas_call(
        merge_kernel,
        in_specs=[vmem] * 4,
        out_specs=vmem,
        out_shape=jax.ShapeDtypeStruct(got.shape, got.dtype),
        compiler_params=pltpu.CompilerParams(vmem_limit_bytes=6 << 20),
        cost_estimate=pl.CostEstimate(
            flops=got.size * 4, transcendentals=got.size // HD, bytes_accessed=got.size * 8
        ),
        name="merge",
    )(mine, my_logs, got, got_logs)


def weight_rows(info, place):
    flip, half, size = place
    row = (info[1] ^ flip) * size
    if half is not None:
        row = row * 2 + (info[2] if half == 0 else 1 - info[2]) * size
    return pl.ds(pl.multiple_of(row, 32), size)


def stage_kernel(info, *rest, places):
    pieces, (weight, sems) = rest[: len(places)], rest[len(places) :]
    copies = [
        pltpu.make_async_copy(piece, weight.at[weight_rows(info, place)], sems.at[i])
        for i, (piece, place) in enumerate(zip(pieces, places))
    ]
    for copy in copies:
        copy.start()
    for copy in copies:
        copy.wait()


def stage(info, pieces, places, depth):
    width = pieces[0].shape[1]
    return pl.pallas_call(
        functools.partial(stage_kernel, places=places),
        in_specs=[pl.BlockSpec(memory_space=pltpu.SMEM)]
        + [pl.BlockSpec(memory_space=pl.ANY)] * len(pieces),
        out_specs=pl.BlockSpec(memory_space=pltpu.VMEM),
        out_shape=jax.ShapeDtypeStruct((depth, width), pieces[0].dtype),
        scratch_shapes=[pltpu.SemaphoreType.DMA((len(pieces),))],
        compiler_params=pltpu.CompilerParams(vmem_limit_bytes=8 << 20),
        cost_estimate=pl.CostEstimate(
            flops=0, transcendentals=0, bytes_accessed=depth * width * 4
        ),
        name="stage",
    )(info, *pieces)


def project_kernel(
    info, a_low, a_high, x_low, x_high, stream, staged, *rest, places
):
    pieces = rest[: len(places)]
    mixed, stream_out, stats, weight, left, sems = rest[len(places) :]
    core = info[0]
    low, high = a_low.shape[1], a_high.shape[1]

    def columns(owner, shift, size):
        return pl.ds(pl.multiple_of(owner * (low + high) + shift, HD), size)

    copies = [
        pltpu.make_async_copy(piece, weight.at[weight_rows(info, place)], sems.at[i])
        for i, (piece, place) in enumerate(zip(pieces, places))
    ]
    for ref, shift in ((x_low, 0), (x_high, low)):
        where = columns(1 - core, shift, ref.shape[1])
        copies.append(pltpu.make_async_copy(ref, left.at[:, where], sems.at[len(copies)]))
    for copy in copies:
        copy.start()
    for ref, shift in ((a_low, 0), (a_high, low)):
        left[:, columns(core, shift, ref.shape[1])] = ref[...]
    for copy in copies:
        copy.wait()
    rows, width = stream.shape
    step = width // 3
    total = jnp.zeros((rows, HD), jnp.float32)
    for first in range(0, width, step):
        block = slice(first, first + step)
        got = jnp.dot(
            left[...], weight[:, block], preferred_element_type=jnp.float32
        ) + stream[:, block].astype(jnp.float32)
        mixed[:, block] = got
        stream_out[:, block] = got.astype(jnp.bfloat16)
        total = total + lane_blocks(got, jnp.add)
    mean = jnp.sum(total, axis=1, keepdims=True) * (1.0 / width)
    square = jnp.zeros((rows, HD), jnp.float32)
    for first in range(0, width, HD):
        off = mixed[:, first : first + HD] - mean
        square = square + off * off
    square = jnp.sum(square, axis=1, keepdims=True)
    lane = lax.broadcasted_iota(jnp.int32, stats.shape, 1)
    stats[...] = jnp.where(lane == 0, mean, square)


def project(info, blocks, stream, staged, pieces, places):
    rows, width = stream.shape
    depth = staged.shape[0]
    vmem = pl.BlockSpec(memory_space=pltpu.VMEM)
    anywhere = pl.BlockSpec(memory_space=pl.ANY)
    return pl.pallas_call(
        functools.partial(project_kernel, places=places),
        in_specs=[pl.BlockSpec(memory_space=pltpu.SMEM)]
        + [vmem] * 2
        + [anywhere] * 2
        + [vmem] * 2
        + [anywhere] * len(pieces),
        out_specs=[vmem] * 4,
        out_shape=[
            jax.ShapeDtypeStruct((rows, width), jnp.float32),
            jax.ShapeDtypeStruct((rows, width), jnp.bfloat16),
            jax.ShapeDtypeStruct((rows, HD), jnp.float32),
            jax.ShapeDtypeStruct(staged.shape, staged.dtype),
        ],
        scratch_shapes=[
            pltpu.VMEM((rows, depth), jnp.bfloat16),
            pltpu.SemaphoreType.DMA((len(pieces) + 2,)),
        ],
        input_output_aliases={6: 3},
        compiler_params=pltpu.CompilerParams(vmem_limit_bytes=14 << 20),
        cost_estimate=pl.CostEstimate(
            flops=2 * rows * depth * width,
            transcendentals=0,
            bytes_accessed=depth * width * 2 + rows * width * 8,
        ),
        name="project",
    )(info, *blocks, stream, staged, *pieces)


def norm_kernel(info, mixed, mine, other, scale, shift, out, held, sems):
    rows, width = mixed.shape
    step = rows // sems.shape[0]
    m0, m1 = mine[:, 0:1], other[:, 0:1]
    q0, q1 = mine[:, 1:2], other[:, 1:2]
    mean = 0.5 * (m0 + m1)
    gap = m0 - m1
    var = (q0 + q1 + gap * gap * (0.5 * width)) * (0.5 / width)
    rate = lax.rsqrt(var + EPS)
    columns = pl.ds(pl.multiple_of(info[0] * width, HD), width)
    gain = 1.0 + scale[:, columns]
    bias = shift[:, columns]
    copies = []
    for first in range(0, rows, step):
        here = slice(first, first + step)
        held[here, :] = ((mixed[here, :] - mean[here]) * rate[here] * gain + bias).astype(
            jnp.bfloat16
        )
        copies.append(
            pltpu.make_async_copy(held.at[here, :], out.at[here, :], sems.at[len(copies)])
        )
        copies[-1].start()
    for copy in copies:
        copy.wait()


def normalize(info, mixed, mine, other, scale_mod, shift_mod):
    rows, width = mixed.shape
    vmem = pl.BlockSpec(memory_space=pltpu.VMEM)
    return pl.pallas_call(
        norm_kernel,
        in_specs=[pl.BlockSpec(memory_space=pltpu.SMEM)] + [vmem] * 5,
        out_specs=pl.BlockSpec(memory_space=pltpu.HBM),
        out_shape=jax.ShapeDtypeStruct((rows, width), jnp.bfloat16),
        scratch_shapes=[
            pltpu.VMEM((rows, width), jnp.bfloat16),
            pltpu.SemaphoreType.DMA((rows // TILE,)),
        ],
        compiler_params=pltpu.CompilerParams(vmem_limit_bytes=12 << 20),
        cost_estimate=pl.CostEstimate(
            flops=6 * rows * width, transcendentals=rows, bytes_accessed=rows * width * 6
        ),
        name="normalize",
    )(info, mixed, mine, other, scale_mod[None, :], shift_mod[None, :])


def on_device_pair(query, key, value, stream, shift_mod, scale_mod, out_weight):
    count = lax.axis_size("seq")
    position = lax.axis_index("seq")
    core = lax.axis_index("head")
    vid = lax.axis_index("video")
    par = position // HT
    height = position % HT
    relayed = jnp.where((height == 1) | (height == 2), 1, 0)

    def flip(x, mask):
        return lax.ppermute(x, "seq", [(i, i ^ mask) for i in range(count)])

    def swap(x, axis):
        return lax.ppermute(x, axis, [(0, 1), (1, 0)])

    def some(x, mask, sources):
        pairs = [(i, i ^ mask) for i in range(count) if i % HT in sources]
        return lax.ppermute(x, "seq", pairs)

    rows_half = out_weight.shape[0] // 2
    w_own = lax.dynamic_slice_in_dim(out_weight, vid * rows_half, rows_half, 0)

    half = query.shape[1] // HD // 2 * HD
    q_low = query[:, :half]
    key, value, late = lax.optimization_barrier((key, value, query, q_low))[:3]
    k_low, v_low = (x[:, :half] for x in (key, value))
    q_high, k_high, v_high = (x[:, half:] for x in (late, key, value))

    e_low = flip(q_low, HT)
    y_kl = flip(k_low, 1)
    v_zl = some(v_low, 2, (1, 2))
    y_vl = flip(v_low, 1)
    w_t = flip(w_own, HT)
    k_fl = some(y_kl, 2, (0, 3))
    v_fl = some(v_zl, 1, (0, 3))
    y_kh = flip(k_high, 1)
    v_zh = some(v_high, 2, (1, 2))
    e_high = flip(q_high, HT)
    y_vh = flip(v_high, 1)
    k_fh = some(y_kh, 2, (0, 3))
    v_fh = some(v_zh, 1, (0, 3))
    w_z1 = flip(w_own, 2)
    w_xd = swap(w_t, "video")
    w_xa = swap(w_z1, "video")
    w_z2 = flip(w_t, 2)
    w_ya = flip(w_own, 1)
    w_yc = flip(w_t, 1)
    w_z3 = flip(w_ya, 2)
    w_yd = flip(w_z2, 1)
    w_xe = swap(w_z2, "video")
    w_xb = swap(w_ya, "video")
    w_yf = flip(w_xd, 1)
    w_xc = swap(w_z3, "video")
    w_xg = swap(w_yd, "video")

    info = jnp.stack([par, relayed]).astype(jnp.int32)
    parts_low = (k_low, v_low, y_kl, y_vl, k_fl, v_fl)
    parts_high = (k_high, v_high, y_kh, y_vh, k_fh, v_fh)
    give_low, logs_low = attention(info, e_low, parts_low, True)
    r_low = flip(give_low, HT)
    l_low = flip(logs_low, HT)
    mine_low, mine_logs_low = attention(info, q_low, parts_low, False)
    give_high, logs_high = attention(info, e_high, parts_high, True)
    r_high = flip(give_high, HT)
    l_high = flip(logs_high, HT)
    mine_high, mine_logs_high = attention(info, q_high, parts_high, False)
    a_low = merge(mine_low, mine_logs_low, r_low, l_low)
    x_low = swap(a_low, "head")
    a_high = merge(mine_high, mine_logs_high, r_high, l_high)
    x_high = swap(a_high, "head")

    n = rows_half
    early = (
        (out_weight, (0, None, 2 * n)),
        (w_z1, (2, 0, n)),
        (w_ya, (1, 0, n)),
        (w_z3, (3, 0, n)),
        (w_t, (4, 0, n)),
        (w_z2, (6, 0, n)),
        (w_yc, (5, 0, n)),
        (w_yd, (7, 0, n)),
        (w_xa, (2, 1, n)),
        (w_xb, (1, 1, n)),
        (w_xd, (4, 1, n)),
        (w_xe, (6, 1, n)),
    )
    last = ((w_xc, (3, 1, n)), (w_yf, (5, 1, n)), (w_xg, (7, 1, n)))
    where = jnp.stack([core, position, vid]).astype(jnp.int32)
    depth = 2 * n * count
    staged = stage(where, *map(tuple, zip(*early)), depth)
    mixed, stream_out, stats, _ = project(
        where, (a_low, a_high, x_low, x_high), stream, staged, *map(tuple, zip(*last))
    )
    other = swap(stats, "head")
    normed = normalize(where, mixed, stats, other, scale_mod, shift_mod)
    return (normed, stream_out)


PAIR = {"video": 2, "seq": 2 * HT, "head": 2}


def on_device(query, *rest):
    sizes = {axis: lax.axis_size(axis) for axis in PAIR}
    if sizes == PAIR:
        return on_device_pair(query, *rest)
    return on_device_any(query, *rest)


def solution(mesh):
    step = jax.shard_map(
        on_device,
        mesh=mesh,
        in_specs=(
            P(("video", "seq"), "head"),
            P(("video", "seq"), "head"),
            P(("video", "seq"), "head"),
            P(("video", "seq"), "head"),
            P("video"),
            P("video"),
            P("seq", "head"),
        ),
        out_specs=(P(("video", "seq"), "head"), P(("video", "seq"), "head")),
        check_vma=False,
    )
    if dict(mesh.shape) != PAIR:
        return step
    return step
```

```python
import functools
import itertools
import math

import jax
import jax.numpy as jnp
from jax import lax
from jax.experimental import pallas as pl
from jax.experimental.pallas import tpu as pltpu
from jax.sharding import PartitionSpec as P


D = 3072
HD = 128
TILE = 128
HT = 4
EPS = 1e-06
EXP2_SCALE = math.log2(math.e) / math.sqrt(HD)
AWAY = -1e30
GROUP = 3


def shifted(value, axis, steps):
    count = lax.axis_size(axis)
    leading, last = (max(0, -steps), min(count, count - steps))
    return lax.ppermute(value, axis, [(source, source + steps) for source in range(leading, last)])


def attend_tile(query_tile, keys_all, values_all, visible):
    tile_rows, features = query_tile.shape
    heads_here = features // HD

    def one_head(head):
        head_query = lax.dynamic_slice_in_dim(query_tile, head * HD, HD, 1)
        head_key = lax.dynamic_slice_in_dim(keys_all, head * HD, HD, 1)
        head_value = lax.dynamic_slice_in_dim(values_all, head * HD, HD, 1)
        scores = jnp.einsum(
            "nd,md->nm", head_query, head_key, preferred_element_type=jnp.float32
        ) / math.sqrt(HD)
        scores = jnp.where(visible[None, :], scores, -jnp.inf)
        top = jnp.max(scores, axis=1, keepdims=True)
        expo = jnp.exp(scores - top)
        total = jnp.sum(expo, axis=1, keepdims=True)
        probs = expo.astype(jnp.bfloat16)
        weighted = jnp.dot(probs, head_value, preferred_element_type=jnp.float32)
        return (weighted / total).astype(jnp.bfloat16)

    per_head = lax.map(one_head, jnp.arange(heads_here, dtype=jnp.int32))
    return jnp.transpose(per_head, (1, 0, 2)).reshape(tile_rows, features)


def on_device_any(query, key, value, stream, shift_mod, scale_mod, out_weight):
    slab_rows = query.shape[0]
    width_tiles = slab_rows // TILE
    layers = lax.axis_size("seq") // HT
    position = lax.axis_index("seq")
    time_tile = position // HT
    height_tile = position % HT
    key_value = jnp.stack([key, value])
    vertical = {0: key_value}
    for offset in (HT, -HT):
        vertical[-offset // HT] = shifted(key_value, "seq", offset)
    column = jnp.stack([vertical[-1], vertical[0], vertical[1]])
    sideways = {0: column}
    for offset in (1, -1):
        sideways[-offset] = shifted(column, "seq", offset)
    neighbours = []
    for across in (-1, 0, 1):
        for upward in (-1, 0, 1):
            inside = (time_tile + across >= 0) & (time_tile + across < layers)
            inside = inside & (height_tile + upward >= 0) & (height_tile + upward < HT)
            neighbours.append((sideways[upward][across + 1], inside))
    results = []
    for tile_pos in range(width_tiles):
        lowest = max(tile_pos - 1, 0)
        highest = min(tile_pos + 1, width_tiles - 1)
        begin = lowest * TILE
        count = (highest - lowest + 1) * TILE
        keys_here = jnp.concatenate(
            [paired[0][begin : begin + count] for paired, inside in neighbours], 0
        )
        values_here = jnp.concatenate(
            [paired[1][begin : begin + count] for paired, inside in neighbours], 0
        )
        flags = jnp.concatenate(
            [jnp.broadcast_to(inside, (count,)) for paired, inside in neighbours]
        )
        query_tile = query[tile_pos * TILE : (tile_pos + 1) * TILE]
        results.append(attend_tile(query_tile, keys_here, values_here, flags))
    attended = jnp.concatenate(results, 0)
    width_cols = D // lax.axis_size("head")
    first_col = lax.axis_index("head") * width_cols
    weight_cols = lax.all_gather(out_weight, "seq", axis=0, tiled=True)
    weight_rows = lax.all_to_all(weight_cols, "head", split_axis=0, concat_axis=1, tiled=True)
    partial_value = jnp.dot(attended, weight_rows, preferred_element_type=jnp.float32)
    share = lax.psum_scatter(partial_value, "head", scatter_dimension=1, tiled=True)
    mixed = stream.astype(jnp.float32) + share
    totals, squares = lax.psum((jnp.sum(mixed, axis=1), jnp.sum(mixed * mixed, axis=1)), "head")
    mean = (totals / D)[:, None]
    var = (squares / D)[:, None] - mean * mean
    scale_part = lax.dynamic_slice_in_dim(scale_mod, first_col, width_cols, 0)
    shift_part = lax.dynamic_slice_in_dim(shift_mod, first_col, width_cols, 0)
    normed = ((mixed - mean) * lax.rsqrt(var + EPS) * (1.0 + scale_part) + shift_part).astype(
        jnp.bfloat16
    )
    return (normed, mixed.astype(jnp.bfloat16))


def lane_blocks(x, op):
    return functools.reduce(op, [x[:, c : c + HD] for c in range(0, x.shape[1], HD)])


def attention_kernel(info, query, *refs, returned):
    out, logs = refs[6:]
    parts = tuple((refs[i], refs[i + 1], i == 4) for i in (0, 2, 4))
    rows = query.shape[0]
    tiles = rows // TILE
    heads = out.shape[1] // HD
    away = jnp.where(info[1] == 1, jnp.float32(0), jnp.float32(AWAY))
    lane = lax.broadcasted_iota(jnp.int32, (TILE, HD), 1)
    log_of = [jnp.zeros((TILE, HD), jnp.float32) for _ in range(tiles)]

    def place(head, tile):
        begin = max(tile - 1, 0) * TILE
        end = (min(tile + 1, tiles - 1) + 1) * TILE
        here = slice(tile * TILE, (tile + 1) * TILE)
        return here, slice(begin, end), slice(head * HD, (head + 1) * HD)

    def score(head, tile):
        here, seen, feats = place(head, tile)
        return [
            lax.dot_general(
                query[here, feats],
                keys[seen, feats],
                (((1,), (1,)), ((), ())),
                preferred_element_type=jnp.float32,
            )
            for keys, _, _ in parts
        ]

    def highest(scores):
        tops = [
            lane_blocks(s, jnp.maximum) + (away if far else 0.0)
            for s, (_, _, far) in zip(scores, parts)
        ]
        return jnp.max(functools.reduce(jnp.maximum, tops), axis=1, keepdims=True)

    def gather(head, tile, scores, top):
        _, seen, feats = place(head, tile)
        acc = jnp.zeros((TILE, HD), jnp.float32)
        total = jnp.zeros((TILE, HD), jnp.float32)
        for s, (_, values, far) in zip(scores, parts):
            p = jnp.exp2((s - (top - away if far else top)) * EXP2_SCALE)
            total = total + lane_blocks(p, jnp.add)
            acc = acc + jnp.dot(
                p.astype(jnp.bfloat16), values[seen, feats], preferred_element_type=jnp.float32
            )
        return acc, jnp.sum(total, axis=1, keepdims=True)

    units = list(itertools.product(range(heads), range(tiles)))
    for start in range(0, len(units), GROUP):
        group = units[start : start + GROUP]
        scores = [score(*unit) for unit in group]
        tops = [highest(s) for s in scores]
        done = [gather(*unit, s, top) for unit, s, top in zip(group, scores, tops)]
        for (head, tile), top, (acc, total) in zip(group, tops, done):
            here, _, feats = place(head, tile)
            out[here, feats] = (acc / total).astype(out.dtype)
            log = top * EXP2_SCALE + jnp.log2(total)
            log_of[tile] = jnp.where(lane == head, log, log_of[tile])
    for tile in range(tiles):
        here = slice(tile * TILE, (tile + 1) * TILE)
        if returned:
            logs[:, here] = jnp.transpose(log_of[tile])[: logs.shape[0], :]
        else:
            logs[here, :] = log_of[tile]


def attention(info, query, parts, returned):
    rows, cols = query.shape
    vmem = pl.BlockSpec(memory_space=pltpu.VMEM)
    pairs = rows * 7 * TILE * cols // HD
    if returned:
        kind, log_shape = jnp.bfloat16, (8, rows)
    else:
        kind, log_shape = jnp.float32, (rows, HD)
    return pl.pallas_call(
        functools.partial(attention_kernel, returned=returned),
        in_specs=[pl.BlockSpec(memory_space=pltpu.SMEM)] + [vmem] * (1 + len(parts)),
        out_specs=[vmem] * 2,
        out_shape=[
            jax.ShapeDtypeStruct((rows, cols), kind),
            jax.ShapeDtypeStruct(log_shape, jnp.float32),
        ],
        compiler_params=pltpu.CompilerParams(vmem_limit_bytes=12 << 20),
        cost_estimate=pl.CostEstimate(
            flops=pairs * HD * 4, transcendentals=pairs, bytes_accessed=rows * cols * 16
        ),
        name="attend",
    )(info, query, *parts)


def merge_kernel(mine, my_logs, got, got_logs, out):
    rows, cols = out.shape
    heads = cols // HD
    for tile in range(rows // TILE):
        here = slice(tile * TILE, (tile + 1) * TILE)
        fill = jnp.zeros((HD - got_logs.shape[0], TILE), jnp.float32)
        other = jnp.transpose(jnp.concatenate([got_logs[:, here], fill], 0))
        logs = my_logs[here, :]
        for head in range(heads):
            feats = slice(head * HD, (head + 1) * HD)
            gap = other[:, head : head + 1] - logs[:, head : head + 1]
            share = 1.0 / (1.0 + jnp.exp2(gap))
            far = got[here, feats].astype(jnp.float32)
            out[here, feats] = (mine[here, feats] * share + far * (1.0 - share)).astype(out.dtype)


def merge(mine, my_logs, got, got_logs):
    vmem = pl.BlockSpec(memory_space=pltpu.VMEM)
    return pl.pallas_call(
        merge_kernel,
        in_specs=[vmem] * 4,
        out_specs=vmem,
        out_shape=jax.ShapeDtypeStruct(got.shape, got.dtype),
        compiler_params=pltpu.CompilerParams(vmem_limit_bytes=6 << 20),
        cost_estimate=pl.CostEstimate(
            flops=got.size * 4, transcendentals=got.size // HD, bytes_accessed=got.size * 8
        ),
        name="merge",
    )(mine, my_logs, got, got_logs)


def weight_rows(info, place):
    flip, half, size = place
    row = (info[1] ^ flip) * size
    if half is not None:
        row = row * 2 + (info[2] if half == 0 else 1 - info[2]) * size
    return pl.ds(pl.multiple_of(row, 32), size)


def stage_kernel(info, *rest, places):
    pieces, (weight, sems) = rest[: len(places)], rest[len(places) :]
    copies = [
        pltpu.make_async_copy(piece, weight.at[weight_rows(info, place)], sems.at[i])
        for i, (piece, place) in enumerate(zip(pieces, places))
    ]
    for copy in copies:
        copy.start()
    for copy in copies:
        copy.wait()


def stage(info, pieces, places, depth):
    width = pieces[0].shape[1]
    return pl.pallas_call(
        functools.partial(stage_kernel, places=places),
        in_specs=[pl.BlockSpec(memory_space=pltpu.SMEM)]
        + [pl.BlockSpec(memory_space=pl.ANY)] * len(pieces),
        out_specs=pl.BlockSpec(memory_space=pltpu.VMEM),
        out_shape=jax.ShapeDtypeStruct((depth, width), pieces[0].dtype),
        scratch_shapes=[pltpu.SemaphoreType.DMA((len(pieces),))],
        compiler_params=pltpu.CompilerParams(vmem_limit_bytes=8 << 20),
        cost_estimate=pl.CostEstimate(
            flops=0, transcendentals=0, bytes_accessed=depth * width * 4
        ),
        name="stage",
    )(info, *pieces)


def project_kernel(
    info, a_low, a_high, x_low, x_high, stream, staged, *rest, places
):
    pieces = rest[: len(places)]
    mixed, stream_out, stats, weight, left, sems = rest[len(places) :]
    core = info[0]
    low, high = a_low.shape[1], a_high.shape[1]

    def columns(owner, shift, size):
        return pl.ds(pl.multiple_of(owner * (low + high) + shift, HD), size)

    copies = [
        pltpu.make_async_copy(piece, weight.at[weight_rows(info, place)], sems.at[i])
        for i, (piece, place) in enumerate(zip(pieces, places))
    ]
    for ref, shift in ((x_low, 0), (x_high, low)):
        where = columns(1 - core, shift, ref.shape[1])
        copies.append(pltpu.make_async_copy(ref, left.at[:, where], sems.at[len(copies)]))
    for copy in copies:
        copy.start()
    for ref, shift in ((a_low, 0), (a_high, low)):
        left[:, columns(core, shift, ref.shape[1])] = ref[...]
    for copy in copies:
        copy.wait()
    rows, width = stream.shape
    step = width // 3
    total = jnp.zeros((rows, HD), jnp.float32)
    for first in range(0, width, step):
        block = slice(first, first + step)
        got = jnp.dot(
            left[...], weight[:, block], preferred_element_type=jnp.float32
        ) + stream[:, block].astype(jnp.float32)
        mixed[:, block] = got
        stream_out[:, block] = got.astype(jnp.bfloat16)
        total = total + lane_blocks(got, jnp.add)
    mean = jnp.sum(total, axis=1, keepdims=True) * (1.0 / width)
    square = jnp.zeros((rows, HD), jnp.float32)
    for first in range(0, width, HD):
        off = mixed[:, first : first + HD] - mean
        square = square + off * off
    square = jnp.sum(square, axis=1, keepdims=True)
    lane = lax.broadcasted_iota(jnp.int32, stats.shape, 1)
    stats[...] = jnp.where(lane == 0, mean, square)


def project(info, blocks, stream, staged, pieces, places):
    rows, width = stream.shape
    depth = staged.shape[0]
    vmem = pl.BlockSpec(memory_space=pltpu.VMEM)
    anywhere = pl.BlockSpec(memory_space=pl.ANY)
    return pl.pallas_call(
        functools.partial(project_kernel, places=places),
        in_specs=[pl.BlockSpec(memory_space=pltpu.SMEM)]
        + [vmem] * 2
        + [anywhere] * 2
        + [vmem] * 2
        + [anywhere] * len(pieces),
        out_specs=[vmem] * 4,
        out_shape=[
            jax.ShapeDtypeStruct((rows, width), jnp.float32),
            jax.ShapeDtypeStruct((rows, width), jnp.bfloat16),
            jax.ShapeDtypeStruct((rows, HD), jnp.float32),
            jax.ShapeDtypeStruct(staged.shape, staged.dtype),
        ],
        scratch_shapes=[
            pltpu.VMEM((rows, depth), jnp.bfloat16),
            pltpu.SemaphoreType.DMA((len(pieces) + 2,)),
        ],
        input_output_aliases={6: 3},
        compiler_params=pltpu.CompilerParams(vmem_limit_bytes=14 << 20),
        cost_estimate=pl.CostEstimate(
            flops=2 * rows * depth * width,
            transcendentals=0,
            bytes_accessed=depth * width * 2 + rows * width * 8,
        ),
        name="project",
    )(info, *blocks, stream, staged, *pieces)


def norm_kernel(info, mixed, mine, other, scale, shift, out, held, sems):
    rows, width = mixed.shape
    step = rows // sems.shape[0]
    m0, m1 = mine[:, 0:1], other[:, 0:1]
    q0, q1 = mine[:, 1:2], other[:, 1:2]
    mean = 0.5 * (m0 + m1)
    gap = m0 - m1
    var = (q0 + q1 + gap * gap * (0.5 * width)) * (0.5 / width)
    rate = lax.rsqrt(var + EPS)
    columns = pl.ds(pl.multiple_of(info[0] * width, HD), width)
    gain = 1.0 + scale[:, columns]
    bias = shift[:, columns]
    copies = []
    for first in range(0, rows, step):
        here = slice(first, first + step)
        held[here, :] = ((mixed[here, :] - mean[here]) * rate[here] * gain + bias).astype(
            jnp.bfloat16
        )
        copies.append(
            pltpu.make_async_copy(held.at[here, :], out.at[here, :], sems.at[len(copies)])
        )
        copies[-1].start()
    for copy in copies:
        copy.wait()


def normalize(info, mixed, mine, other, scale_mod, shift_mod):
    rows, width = mixed.shape
    vmem = pl.BlockSpec(memory_space=pltpu.VMEM)
    return pl.pallas_call(
        norm_kernel,
        in_specs=[pl.BlockSpec(memory_space=pltpu.SMEM)] + [vmem] * 5,
        out_specs=pl.BlockSpec(memory_space=pltpu.HBM),
        out_shape=jax.ShapeDtypeStruct((rows, width), jnp.bfloat16),
        scratch_shapes=[
            pltpu.VMEM((rows, width), jnp.bfloat16),
            pltpu.SemaphoreType.DMA((rows // TILE,)),
        ],
        compiler_params=pltpu.CompilerParams(vmem_limit_bytes=12 << 20),
        cost_estimate=pl.CostEstimate(
            flops=6 * rows * width, transcendentals=rows, bytes_accessed=rows * width * 6
        ),
        name="normalize",
    )(info, mixed, mine, other, scale_mod[None, :], shift_mod[None, :])


def on_device_pair(query, key, value, stream, shift_mod, scale_mod, out_weight):
    count = lax.axis_size("seq")
    position = lax.axis_index("seq")
    core = lax.axis_index("head")
    vid = lax.axis_index("video")
    par = position // HT
    height = position % HT
    relayed = jnp.where((height == 1) | (height == 2), 1, 0)

    def flip(x, mask):
        return lax.ppermute(x, "seq", [(i, i ^ mask) for i in range(count)])

    def swap(x, axis):
        return lax.ppermute(x, axis, [(0, 1), (1, 0)])

    def some(x, mask, sources):
        pairs = [(i, i ^ mask) for i in range(count) if i % HT in sources]
        return lax.ppermute(x, "seq", pairs)

    rows_half = out_weight.shape[0] // 2
    w_own = lax.dynamic_slice_in_dim(out_weight, vid * rows_half, rows_half, 0)

    half = query.shape[1] // HD // 2 * HD
    q_low = query[:, :half]
    key, value, late = lax.optimization_barrier((key, value, query, q_low))[:3]
    k_low, v_low = (x[:, :half] for x in (key, value))
    q_high, k_high, v_high = (x[:, half:] for x in (late, key, value))

    e_low = flip(q_low, HT)
    y_kl = flip(k_low, 1)
    v_zl = some(v_low, 2, (1, 2))
    y_vl = flip(v_low, 1)
    w_t = flip(w_own, HT)
    k_fl = some(y_kl, 2, (0, 3))
    v_fl = some(v_zl, 1, (0, 3))
    y_kh = flip(k_high, 1)
    v_zh = some(v_high, 2, (1, 2))
    e_high = flip(q_high, HT)
    y_vh = flip(v_high, 1)
    k_fh = some(y_kh, 2, (0, 3))
    v_fh = some(v_zh, 1, (0, 3))
    w_z1 = flip(w_own, 2)
    w_xd = swap(w_t, "video")
    w_xa = swap(w_z1, "video")
    w_z2 = flip(w_t, 2)
    w_ya = flip(w_own, 1)
    w_yc = flip(w_t, 1)
    w_z3 = flip(w_ya, 2)
    w_yd = flip(w_z2, 1)
    w_xe = swap(w_z2, "video")
    w_xb = swap(w_ya, "video")
    w_xf = swap(w_yc, "video")
    w_yx = flip(w_xa, 1)
    w_xg = swap(w_yd, "video")

    info = jnp.stack([par, relayed]).astype(jnp.int32)
    parts_low = (k_low, v_low, y_kl, y_vl, k_fl, v_fl)
    parts_high = (k_high, v_high, y_kh, y_vh, k_fh, v_fh)
    give_low, logs_low = attention(info, e_low, parts_low, True)
    r_low = flip(give_low, HT)
    l_low = flip(logs_low, HT)
    mine_low, mine_logs_low = attention(info, q_low, parts_low, False)
    give_high, logs_high = attention(info, e_high, parts_high, True)
    r_high = flip(give_high, HT)
    l_high = flip(logs_high, HT)
    mine_high, mine_logs_high = attention(info, q_high, parts_high, False)
    a_low = merge(mine_low, mine_logs_low, r_low, l_low)
    x_low = swap(a_low, "head")
    a_high = merge(mine_high, mine_logs_high, r_high, l_high)
    x_high = swap(a_high, "head")

    n = rows_half
    early = (
        (out_weight, (0, None, 2 * n)),
        (w_z1, (2, 0, n)),
        (w_ya, (1, 0, n)),
        (w_z3, (3, 0, n)),
        (w_t, (4, 0, n)),
        (w_z2, (6, 0, n)),
        (w_yc, (5, 0, n)),
        (w_yd, (7, 0, n)),
        (w_xa, (2, 1, n)),
        (w_xb, (1, 1, n)),
        (w_xd, (4, 1, n)),
        (w_xe, (6, 1, n)),
        (w_xf, (5, 1, n)),
    )
    last = ((w_yx, (3, 1, n)), (w_xg, (7, 1, n)))
    where = jnp.stack([core, position, vid]).astype(jnp.int32)
    depth = 2 * n * count
    staged = stage(where, *map(tuple, zip(*early)), depth)
    mixed, stream_out, stats, _ = project(
        where, (a_low, a_high, x_low, x_high), stream, staged, *map(tuple, zip(*last))
    )
    other = swap(stats, "head")
    normed = normalize(where, mixed, stats, other, scale_mod, shift_mod)
    return (normed, stream_out)


PAIR = {"video": 2, "seq": 2 * HT, "head": 2}


def on_device(query, *rest):
    sizes = {axis: lax.axis_size(axis) for axis in PAIR}
    if sizes == PAIR:
        return on_device_pair(query, *rest)
    return on_device_any(query, *rest)


def solution(mesh):
    step = jax.shard_map(
        on_device,
        mesh=mesh,
        in_specs=(
            P(("video", "seq"), "head"),
            P(("video", "seq"), "head"),
            P(("video", "seq"), "head"),
            P(("video", "seq"), "head"),
            P("video"),
            P("video"),
            P("seq", "head"),
        ),
        out_specs=(P(("video", "seq"), "head"), P(("video", "seq"), "head")),
        check_vma=False,
    )
    if dict(mesh.shape) != PAIR:
        return step
    return step
```
